1024 devices in a mesh: energy: 32 (over y, z_lo), momentum: 32 (over x, z_hi, core).
Axes of the slice: x: 4, y: 4, z: 32 (z_hi: 4, z_lo: 8; z = z_hi * 8 + z_lo), core: 2. Of those that a mesh axis runs over, the one named last changes fastest.
Arguments:
- device_hamiltonian: float32 [32, 2, 256, 256], P('momentum'), may hold values from -3 to 1, as said below
- lead_hamiltonian: float32 [32, 2, 256, 256], P('momentum'), may hold values from -3 to 1, as said below
- lead_coupling: float32 [32, 2, 256, 256], P('momentum'), may hold values from -0.28 to 0.28
- pair_atoms: int32 [2, 128], replicated, may hold values from 0 to 20, as said below
- phonon_shift: int32 [4], replicated, may hold values from 1 to 31
- occupation: float32 [4], replicated, may hold values from 0.2 to 1.5
- phonon_coupling: float32 [4, 128], replicated, may hold values from 0.1 to 0.4
Outputs:
- green_final: float32 [32, 32, 2, 256, 256], P('energy', 'momentum')
The draws below stay inside these ranges and needn't reach their ends.
Inputs may be any that keep to these rules, and one draw needn't show every extreme that they name: `device_hamiltonian`: each diagonal entry has its real part in [-1, 1] and its imaginary part in [-3, -1.5]; off-diagonal entries lie within 0.21 in magnitude. `lead_hamiltonian`: each diagonal entry has its real part in [-1, 1] and its imaginary part in [-3, -1.5]; off-diagonal entries lie within 0.12 in magnitude. `pair_atoms`: the first 21 pairs join each atom with itself, in order; every other pair joins two different atoms.
All inputs are finite; a program needn't handle non-finite values.
Results may differ from the reference program's by a relative error of at most 0.00011.
Values sent between devices are 32-bit elements; how exact they have to be, the bound alone decides.
No kernel may reach another device: no remote copies, remote signals or barrier semaphores. Data moves between devices by JAX's collectives and lax.ppermute only.
A program may use at most 64 MiB of HBM per device.

```python
import math
import jax
import jax.numpy as jnp
from jax import lax

B = 256
ORB = 12
ATOMS = 21
PAIRS = 128
MODES = 4
NEWTON = 2
E_ALL = 32
MOMENTA = 32


def pair_list(key):
    first_key, offset_key = jax.random.split(jax.random.fold_in(key, 37))
    extra_pairs = PAIRS - ATOMS
    first_atoms = jax.random.randint(first_key, (extra_pairs,), 0, ATOMS, dtype=jnp.int32)
    offsets = jax.random.randint(offset_key, (extra_pairs,), 1, ATOMS, dtype=jnp.int32)
    second_atoms = (first_atoms + offsets) % ATOMS
    own_atoms = jnp.arange(ATOMS, dtype=jnp.int32)
    return jnp.stack([jnp.concatenate([own_atoms, first_atoms]), jnp.concatenate([own_atoms, second_atoms])]).astype(jnp.int32)


def neighbour_blocks(key, pairs):
    real_key, imag_key = jax.random.split(jax.random.fold_in(key, 53))
    atom_rows = ATOMS * ORB
    shape = (atom_rows, atom_rows)
    real_part = 0.05 * jnp.clip(jax.random.normal(real_key, shape, jnp.float32), -3.0, 3.0)
    imag_part = 0.025 * jnp.clip(jax.random.normal(imag_key, shape, jnp.float32), -3.0, 3.0)
    occupied = jnp.zeros((ATOMS, ATOMS), jnp.float32).at[pairs[0], pairs[1]].set(1.0)
    spread_mask = jnp.broadcast_to(occupied[:, None, :, None], (ATOMS, ORB, ATOMS, ORB)).reshape(atom_rows, atom_rows)
    spread_mask = spread_mask * (1.0 - jnp.eye(atom_rows, dtype=jnp.float32))
    spare_rows = B - atom_rows
    padding = ((0, spare_rows), (0, spare_rows))
    return (jnp.pad(real_part * spread_mask, padding), jnp.pad(imag_part * spread_mask, padding))


def random_slab(key):
    noise_key, onsite_key, absorb_key = jax.random.split(key, 3)
    shape = (MOMENTA, 2, B, B)
    spread = 0.02 * jnp.clip(jax.random.normal(noise_key, shape, jnp.float32), -6.0, 6.0)
    identity = jnp.eye(B, dtype=jnp.float32)
    onsite = jax.random.uniform(onsite_key, (MOMENTA, B), jnp.float32, -1.0, 1.0)
    absorb = jax.random.uniform(absorb_key, (MOMENTA, B), jnp.float32, 1.5, 3.0)
    real_part = spread[:, 0] * (1.0 - identity) + onsite[:, :, None] * identity
    imag_part = spread[:, 1] * (1.0 - identity) - absorb[:, :, None] * identity
    return jnp.stack([real_part, imag_part], axis=1)


def device_slab(key):
    noise_key, onsite_key, absorb_key, moving_key, damping_key = jax.random.split(jax.random.fold_in(key, 11), 5)
    shape = (MOMENTA, 2, B, B)
    spread = 0.01 * jnp.clip(jax.random.normal(noise_key, shape, jnp.float32), -6.0, 6.0)
    identity = jnp.eye(B, dtype=jnp.float32)
    onsite = jax.random.uniform(onsite_key, (B,), jnp.float32, -0.7, 0.7)[None, :] + jax.random.uniform(moving_key, (MOMENTA, B), jnp.float32, -0.3, 0.3)
    absorb = jax.random.uniform(absorb_key, (B,), jnp.float32, 1.5, 2.7)[None, :] + jax.random.uniform(damping_key, (MOMENTA, B), jnp.float32, 0.0, 0.3)
    neighbour_real, neighbour_imag = neighbour_blocks(key, pair_list(key))
    real_part = spread[:, 0] * (1.0 - identity) + neighbour_real[None] + onsite[:, :, None] * identity
    imag_part = spread[:, 1] * (1.0 - identity) + neighbour_imag[None] - absorb[:, :, None] * identity
    return jnp.stack([real_part, imag_part], axis=1)


def draw_device_hamiltonian(key, part):
    return device_slab(key)


def draw_lead_hamiltonian(key, part):
    return random_slab(jax.random.fold_in(key, 23))


def draw_lead_coupling(key, part):
    shape = (MOMENTA, 2, B, B)
    noise = jax.random.normal(jax.random.fold_in(key, 71), shape, jnp.float32)
    coupling = 0.035 * jnp.clip(noise, -8.0, 8.0)
    return coupling


def draw_pair_atoms(key, part):
    return pair_list(key)


def touch_ends(values, key, least, top_value):
    longest = values.shape.index(max(values.shape))
    spots = []
    for shift in (0, 1):
        where = [jax.random.randint(jax.random.fold_in(key, axis), (), 0, length) for axis, length in enumerate(values.shape)]
        where[longest] = (where[longest] + shift) % values.shape[longest]
        spots.append(tuple(where))
    return values.at[spots[0]].set(least).at[spots[1]].set(top_value)


def setup_inputs(seed: int = 0) -> dict:
    keys = jax.random.split(jax.random.key(seed), 8)
    return {
        "device_hamiltonian": draw_device_hamiltonian(jax.random.fold_in(keys[7], 71), 0),
        "lead_hamiltonian": draw_lead_hamiltonian(jax.random.fold_in(keys[7], 71), 0),
        "lead_coupling": draw_lead_coupling(jax.random.fold_in(keys[7], 71), 0),
        "pair_atoms": draw_pair_atoms(jax.random.fold_in(keys[7], 71), 0),
        "phonon_shift": touch_ends(jax.random.randint(keys[4], (MODES,), 1, E_ALL), jax.random.fold_in(keys[4], 1), 1, E_ALL - 1).astype(jnp.int32),
        "occupation": jnp.clip(jnp.exp(jax.random.uniform(keys[5], (MODES,), jnp.float32, math.log(0.2), math.log(1.5))), 0.2, 1.5),
        "phonon_coupling": jnp.clip(jax.random.uniform(keys[6], (MODES, PAIRS), jnp.float32, 0.1, 0.4), 0.1, 0.4),
    }


HIGHEST_PRECISION = lax.Precision.HIGHEST


def complex_product(left_factor, right_factor):
    left_real = left_factor[..., 0, :, :]
    left_imag = left_factor[..., 1, :, :]
    right_real = right_factor[..., 0, :, :]
    right_imag = right_factor[..., 1, :, :]
    real_part = jnp.matmul(left_real, right_real, precision=HIGHEST_PRECISION) - jnp.matmul(left_imag, right_imag, precision=HIGHEST_PRECISION)
    imag_part = jnp.matmul(left_real, right_imag, precision=HIGHEST_PRECISION) + jnp.matmul(left_imag, right_real, precision=HIGHEST_PRECISION)
    return jnp.stack([real_part, imag_part], axis=-3)


def make_system(energy, hamiltonian):
    identity = jnp.eye(hamiltonian.shape[-1], dtype=jnp.float32)
    real_part = energy[:, None, None, None] * identity - hamiltonian[None, :, 0]
    imag_part = jnp.zeros_like(real_part) - hamiltonian[None, :, 1]
    return jnp.stack([real_part, imag_part], axis=2)


def diagonal_step(system, bare_system):
    diag_real = jnp.diagonal(bare_system[..., 0, :, :], axis1=-2, axis2=-1)
    diag_imag = jnp.diagonal(bare_system[..., 1, :, :], axis1=-2, axis2=-1)
    modulus = diag_real * diag_real + diag_imag * diag_imag
    inverse_real = diag_real / modulus
    inverse_imag = -diag_imag / modulus
    system_real = system[..., 0, :, :]
    system_imag = system[..., 1, :, :]
    column_real = system_real * inverse_real[..., None, :] - system_imag * inverse_imag[..., None, :]
    column_imag = system_real * inverse_imag[..., None, :] + system_imag * inverse_real[..., None, :]
    both_real = inverse_real[..., :, None] * column_real - inverse_imag[..., :, None] * column_imag
    both_imag = inverse_real[..., :, None] * column_imag + inverse_imag[..., :, None] * column_real
    identity = jnp.eye(system.shape[-1], dtype=jnp.float32)
    start_real = 2.0 * identity * inverse_real[..., None, :] - both_real
    start_imag = 2.0 * identity * inverse_imag[..., None, :] - both_imag
    return jnp.stack([start_real, start_imag], axis=-3)


def newton(system, initial, repeats):
    current = initial
    for repeat_index in range(repeats):
        residual = complex_product(system, current)
        current = 2.0 * current - complex_product(current, residual)
    return current


def first_round(energy, device_hamiltonian, lead_hamiltonian, lead_coupling):
    lead_system = make_system(energy, lead_hamiltonian)
    green_lead = newton(lead_system, diagonal_step(lead_system, lead_system), NEWTON)
    contact = complex_product(complex_product(lead_coupling, green_lead), jnp.swapaxes(lead_coupling, -1, -2))
    bare_system = make_system(energy, device_hamiltonian)
    device_system = bare_system - contact
    green_device = newton(device_system, diagonal_step(device_system, bare_system), NEWTON)
    return device_system, green_device


def pair_sums(green_device, pair_atoms):
    atom_rows = ATOMS * ORB
    trimmed = green_device[..., :atom_rows, :atom_rows]
    shaped = trimmed.reshape(trimmed.shape[:3] + (ATOMS, ORB, ATOMS, ORB))
    selected = shaped[:, :, :, pair_atoms[0], :, pair_atoms[1], :]
    summed = jnp.sum(selected, axis=2)
    return jnp.transpose(summed, (1, 2, 3, 4, 0)).reshape(summed.shape[1], 2 * ORB * ORB, summed.shape[0])


def convolve(blocks, phonon_shift, occupation, phonon_coupling):
    energy_count = blocks.shape[0]
    source_index = jnp.arange(energy_count, dtype=jnp.int32)[:, None]
    target_index = jnp.arange(energy_count, dtype=jnp.int32)[None, :]
    flattened = blocks.reshape(energy_count, -1)
    result = jnp.zeros(blocks.shape, jnp.float32)
    for phonon_mode in range(MODES):
        shift_value = phonon_shift[phonon_mode]
        below = (source_index == target_index - shift_value).astype(jnp.float32)
        above = (source_index == target_index + shift_value).astype(jnp.float32)
        kernel = occupation[phonon_mode] * below + (occupation[phonon_mode] + 1.0) * above
        shifted = jnp.dot(kernel.T, flattened, precision=HIGHEST_PRECISION).reshape(blocks.shape)
        result = result + shifted * phonon_coupling[phonon_mode][None, None, :]
    return result


def place_pairs(self_energy, pair_atoms):
    energy_count = self_energy.shape[0]
    values = jnp.transpose(self_energy.reshape(energy_count, 2, ORB, ORB, -1), (4, 0, 1, 2, 3))
    canvas = jnp.zeros((energy_count, 2, ATOMS, ORB, ATOMS, ORB), jnp.float32)
    canvas = canvas.at[:, :, pair_atoms[0], :, pair_atoms[1], :].add(values)
    atom_rows = ATOMS * ORB
    matrix = canvas.reshape(energy_count, 2, atom_rows, atom_rows)
    spare_rows = B - atom_rows
    return jnp.pad(matrix, ((0, 0), (0, 0), (0, spare_rows), (0, spare_rows)))


def reference(device_hamiltonian, lead_hamiltonian, lead_coupling, pair_atoms, phonon_shift, occupation, phonon_coupling):
    energies = -1.0 + 2.0 * (jnp.arange(E_ALL, dtype=jnp.float32) + 0.5) / E_ALL

    def gather_blocks(energy):
        device_system, green_device = first_round(energy[None], device_hamiltonian, lead_hamiltonian, lead_coupling)
        return pair_sums(green_device, pair_atoms)[0]

    averaged = lax.map(gather_blocks, energies) / MOMENTA
    self_energy = convolve(averaged, phonon_shift, occupation, phonon_coupling)

    def second_round(inputs):
        energy, own_energy = inputs
        device_system, green_device = first_round(energy[None], device_hamiltonian, lead_hamiltonian, lead_coupling)
        second_system = device_system - place_pairs(own_energy[None], pair_atoms)[:, None]
        return newton(second_system, green_device, NEWTON)[0]

    return lax.map(second_round, (energies, self_energy))
```

```python
import jax
import jax.numpy as jnp
from jax import lax
from jax.experimental import pallas as pl
from jax.experimental.pallas import tpu as pltpu
from jax.sharding import Mesh
from jax.sharding import PartitionSpec as P

B = 256
ORB = 12
ATOMS = 21
PAIRS = 128
MODES = 4
MOMENTA = 32
ROWS = 2 * ORB * ORB
HALVES = (ATOMS + 1) // 2

INTERPRET = False


def split(value):
    high = value.astype(jnp.bfloat16)
    low = (value - high.astype(jnp.float32)).astype(jnp.bfloat16)
    return high, low


def split_complex(real, imag):
    real_high, real_low = split(real)
    imag_high, imag_low = split(imag)
    return real_high, real_low, imag_high, imag_low


def left_factors(parts):
    real_high, real_low, imag_high, imag_low = parts
    plain = [real_high, real_high, real_low]
    turned = [imag_high, imag_high, imag_low]
    minus = [-imag_high, -imag_high, -imag_low]
    return (
        jnp.concatenate(plain + minus, axis=1),
        jnp.concatenate(plain + turned, axis=1),
    )


def dot(left, right):
    return lax.dot_general(
        left, right, (((1,), (0,)), ((), ())), preferred_element_type=jnp.float32
    )


def dot_transposed(left, right):
    return lax.dot_general(
        left, right, (((1,), (1,)), ((), ())), preferred_element_type=jnp.float32
    )


def times(left, right_parts, transposed=False):
    for_real, for_imag = left
    real_high, real_low, imag_high, imag_low = right_parts
    axis = 1 if transposed else 0
    product = dot_transposed if transposed else dot
    real_right = jnp.concatenate(
        [real_high, real_low, real_high, imag_high, imag_low, imag_high], axis=axis
    )
    imag_right = jnp.concatenate(
        [imag_high, imag_low, imag_high, real_high, real_low, real_high], axis=axis
    )
    return product(for_real, real_right), product(for_imag, imag_right)


def add(left, right):
    return left[0] + right[0], left[1] + right[1]


def grid_of(axis, shape=(B, B)):
    return lax.broadcasted_iota(jnp.int32, shape, axis)


def inverse_of(system, bare):
    system_real, system_imag = system
    bare_real, bare_imag = bare
    identity = (grid_of(0) == grid_of(1)).astype(jnp.float32)
    diag_real = jnp.sum(bare_real * identity, axis=0, keepdims=True)
    diag_imag = jnp.sum(bare_imag * identity, axis=0, keepdims=True)
    modulus = diag_real * diag_real + diag_imag * diag_imag
    row_real = diag_real / modulus
    row_imag = -diag_imag / modulus
    column_real = jnp.sum(identity * row_real, axis=1, keepdims=True)
    column_imag = jnp.sum(identity * row_imag, axis=1, keepdims=True)
    error_real = identity - (column_real * system_real - column_imag * system_imag)
    error_imag = -(column_real * system_imag + column_imag * system_real)
    plus_real = identity + error_real
    start = (
        plus_real * row_real - error_imag * row_imag,
        plus_real * row_imag + error_imag * row_real,
    )
    error_parts = split_complex(error_real, error_imag)
    squared = times(left_factors(error_parts), error_parts)
    return two_more(squared, start)


def two_more(squared, start):
    squared_parts = split_complex(*squared)
    squared_left = left_factors(squared_parts)
    first = add(start, times(squared_left, split_complex(*start)))
    fourth = times(squared_left, squared_parts)
    fourth_left = left_factors(split_complex(*fourth))
    return add(first, times(fourth_left, split_complex(*first)))


def first_kernel(
    energy_ref, device_ref, lead_ref, coupling_ref, pair_ref, system_ref, green_ref, blocks_ref, rows_ref
):
    energy = energy_ref[0]
    scaled_identity = jnp.where(grid_of(0) == grid_of(1), energy, 0.0)
    lead = (scaled_identity - lead_ref[0, 0], -lead_ref[0, 1])
    green_lead = inverse_of(lead, lead)
    coupling_parts = split_complex(coupling_ref[0, 0], coupling_ref[0, 1])
    half = times(left_factors(coupling_parts), split_complex(*green_lead))
    contact = times(left_factors(split_complex(*half)), coupling_parts, transposed=True)
    bare = (scaled_identity - device_ref[0, 0], -device_ref[0, 1])
    system = (bare[0] - contact[0], bare[1] - contact[1])
    system_ref[0] = system[0]
    system_ref[1] = system[1]
    green = inverse_of(system, bare)
    green_ref[0] = green[0]
    green_ref[1] = green[1]
    take_blocks(green, pair_ref, rows_ref)
    shards, shard_rows = blocks_ref.shape[:2]
    for shard in range(shards):
        blocks_ref[shard] = rows_ref[shard * shard_rows : (shard + 1) * shard_rows, :]


def take_blocks(green, pair_ref, rows_ref):
    real_high, real_low = split(green[0])
    imag_high, imag_low = split(green[1])
    left = jnp.concatenate(
        [
            jnp.concatenate([real_high, real_low], axis=1),
            jnp.concatenate([imag_high, imag_low], axis=1),
        ],
        axis=0,
    )
    row_atom = pair_ref[0:1, :]
    column_atom = pair_ref[1:2, :]
    row_half = row_atom // 2
    row_odd = (row_atom - 2 * row_half) == 1
    row_half = jnp.concatenate([row_half, row_half], axis=1)
    row_odd = jnp.concatenate([row_atom, row_atom], axis=1) - 2 * row_half == 1
    offset = grid_of(0, (B, PAIRS)) - ORB * column_atom
    for first in range(0, ORB, 2):
        pick = jnp.concatenate(
            [(offset == first).astype(jnp.bfloat16), (offset == first + 1).astype(jnp.bfloat16)],
            axis=1,
        )
        columns = dot(left, jnp.concatenate([pick, pick], axis=0))
        for part in range(2):
            found = jnp.zeros((2 * ORB, 2 * PAIRS), jnp.float32)
            for half in range(HALVES):
                begin = part * B + 2 * ORB * half
                if half == HALVES - 1:
                    piece = jnp.concatenate(
                        [columns[begin : begin + 16], jnp.zeros((8, 2 * PAIRS), jnp.float32)], axis=0
                    )
                else:
                    piece = columns[begin : begin + 2 * ORB]
                found = jnp.where(row_half == half, piece, found)
            chosen = jnp.where(row_odd, found[ORB:], found[:ORB])
            for side in range(2):
                row = (part * ORB + first + side) * ORB
                rows_ref[row : row + ORB, :] = chosen[:, side * PAIRS : (side + 1) * PAIRS]


def place_blocks(values, pair_ref):
    row_atom = pair_ref[0:1, :]
    column_atom = pair_ref[1:2, :]
    row_half = row_atom // 2
    row_odd = row_atom - 2 * row_half
    identity = grid_of(0, (PAIRS, PAIRS)) == grid_of(1, (PAIRS, PAIRS))
    column_of = jnp.sum(
        jnp.where(identity, (ORB * column_atom).astype(jnp.float32), 0.0), axis=1, keepdims=True
    ).astype(jnp.int32)
    offset = grid_of(1, (PAIRS, B)) - column_of
    pick = jnp.concatenate(
        [(offset == column).astype(jnp.bfloat16) for column in range(ORB)], axis=0
    )
    results = []
    for part in range(2):
        highs = []
        lows = []
        for column in range(ORB):
            row = (part * ORB + column) * ORB
            block = values[row : row + ORB, :]
            both = jnp.concatenate(
                [jnp.where(row_odd == 0, block, 0.0), jnp.where(row_odd == 1, block, 0.0)], axis=0
            )
            pieces = []
            for half in range(HALVES):
                piece = jnp.where(row_half == half, both, 0.0)
                pieces.append(piece[:16] if half == HALVES - 1 else piece)
            spread = jnp.concatenate(pieces, axis=0)
            high, low = split(spread)
            highs.append(high)
            lows.append(low)
        left = jnp.concatenate(highs + lows, axis=1)
        results.append(dot(left, jnp.concatenate([pick, pick], axis=0)))
    return results


def last_kernel(system_ref, green_ref, blocks_ref, pair_ref, out_ref):
    shards, shard_rows = blocks_ref.shape[:2]
    values = jnp.concatenate([blocks_ref[shard] for shard in range(shards)], axis=0)
    scattering = place_blocks(values, pair_ref)
    second = (system_ref[0] - scattering[0], system_ref[1] - scattering[1])
    green = (green_ref[0], green_ref[1])
    identity = (grid_of(0) == grid_of(1)).astype(jnp.float32)
    product = times(left_factors(split_complex(*green)), split_complex(*second))
    residual = (identity - product[0], -product[1])
    final = two_more(residual, green)
    out_ref[0, 0, 0] = final[0]
    out_ref[0, 0, 1] = final[1]


def vmem(count):
    return [pl.BlockSpec(memory_space=pltpu.VMEM)] * count


def first_call(energy, device_hamiltonian, lead_hamiltonian, lead_coupling, pair_atoms, shards):
    shape = jax.ShapeDtypeStruct((2, B, B), jnp.float32)
    blocks = jax.ShapeDtypeStruct((shards, ROWS // shards, PAIRS), jnp.float32)
    return pl.pallas_call(
        first_kernel,
        out_shape=(shape, shape, blocks),
        in_specs=[pl.BlockSpec(memory_space=pltpu.SMEM)] + vmem(4),
        out_specs=tuple(vmem(3)),
        scratch_shapes=[pltpu.VMEM((ROWS, PAIRS), jnp.float32)],
        name="first_round",
        interpret=INTERPRET,
    )(energy, device_hamiltonian, lead_hamiltonian, lead_coupling, pair_atoms)


def last_call(system, green, blocks, pair_atoms):
    return pl.pallas_call(
        last_kernel,
        out_shape=jax.ShapeDtypeStruct((1, 1, 2, B, B), jnp.float32),
        in_specs=vmem(4),
        out_specs=pl.BlockSpec(memory_space=pltpu.VMEM),
        name="second_round",
        interpret=INTERPRET,
    )(system, green, blocks, pair_atoms)


def exchange(array, axes):
    return lax.all_to_all(array, axes, split_axis=0, concat_axis=0, tiled=True)


def slab_sum_kernel(arrived_ref, out_ref, sums_ref):
    groups, rows = sums_ref.shape[0] // arrived_ref.shape[1], arrived_ref.shape[1]
    members = arrived_ref.shape[0] // groups
    for group in range(groups):
        total = arrived_ref[group * members]
        for member in range(1, members):
            total = total + arrived_ref[group * members + member]
        sums_ref[group * rows : (group + 1) * rows, :] = total
    for copy in range(out_ref.shape[0]):
        out_ref[copy] = sums_ref[...]


def column_sum_kernel(arrived_ref, out_ref):
    total = arrived_ref[0]
    for member in range(1, arrived_ref.shape[0]):
        total = total + arrived_ref[member]
    for copy in range(out_ref.shape[0]):
        out_ref[copy] = total


def convolve_kernel(lane_ref, shift_ref, occupation_ref, coupling_ref, arrived_ref, out_ref):
    lanes, stacked = arrived_ref.shape[:2]
    rows = out_ref.shape[1]
    planes = stacked // rows
    copies = out_ref.shape[0] // planes
    energies = lanes * planes
    source = lax.broadcasted_iota(jnp.int32, (energies, PAIRS), 0)
    weights = []
    for plane in range(planes):
        target = plane * lanes + lane_ref[0]
        total = jnp.zeros((energies, PAIRS), jnp.float32)
        for mode in range(MODES):
            occupied = occupation_ref[mode]
            shift = shift_ref[mode]
            factor = jnp.where(source == target - shift, occupied, 0.0) + jnp.where(
                source == target + shift, occupied + 1.0, 0.0
            )
            total = total + factor * coupling_ref[mode : mode + 1, :]
        weights.append(total / MOMENTA)
    results = [jnp.zeros((rows, PAIRS), jnp.float32) for _ in range(planes)]
    for lane in range(lanes):
        for plane in range(planes):
            piece = arrived_ref[lane, plane * rows : (plane + 1) * rows, :]
            energy = plane * lanes + lane
            for target in range(planes):
                results[target] = results[target] + weights[target][energy : energy + 1, :] * piece
    for plane in range(planes):
        for copy in range(copies):
            out_ref[plane * copies + copy] = results[plane]


def per_device(
    device_hamiltonian,
    lead_hamiltonian,
    lead_coupling,
    pair_atoms,
    phonon_shift,
    occupation,
    phonon_coupling,
):
    planes = lax.axis_size("y")
    lanes = lax.axis_size("z_lo")
    columns = lax.axis_size("z_hi")
    slab = planes * lax.axis_size("x") * lax.axis_size("core")
    rows = ROWS // slab
    energy_index = lax.axis_index(("y", "z_lo"))
    energy = -1.0 + 2.0 * (energy_index.astype(jnp.float32) + 0.5) / (planes * lanes)
    system, green, blocks = first_call(
        energy[None], device_hamiltonian, lead_hamiltonian, lead_coupling, pair_atoms, slab
    )
    arrived = exchange(blocks, ("y", "x", "core"))
    summed = pl.pallas_call(
        slab_sum_kernel,
        out_shape=jax.ShapeDtypeStruct((columns, planes * rows, PAIRS), jnp.float32),
        in_specs=vmem(1),
        out_specs=vmem(1)[0],
        scratch_shapes=[pltpu.VMEM((planes * rows, PAIRS), jnp.float32)],
        name="slab_sum",
        interpret=INTERPRET,
    )(arrived)
    arrived = exchange(summed, "z_hi")
    summed = pl.pallas_call(
        column_sum_kernel,
        out_shape=jax.ShapeDtypeStruct((lanes, planes * rows, PAIRS), jnp.float32),
        in_specs=vmem(1),
        out_specs=vmem(1)[0],
        name="column_sum",
        interpret=INTERPRET,
    )(arrived)
    arrived = exchange(summed, "z_lo")
    self_energy = pl.pallas_call(
        convolve_kernel,
        out_shape=jax.ShapeDtypeStruct((slab, rows, PAIRS), jnp.float32),
        in_specs=[pl.BlockSpec(memory_space=pltpu.SMEM)] * 3 + vmem(2),
        out_specs=vmem(1)[0],
        name="phonon_sum",
        interpret=INTERPRET,
    )(lax.axis_index("z_lo")[None], phonon_shift, occupation, phonon_coupling, arrived)
    arrived = exchange(self_energy, ("y", "x", "core"))
    return last_call(system, green, arrived, pair_atoms)


def solution(mesh):
    momentum = ("x", "z_hi", "core")
    split_mesh = Mesh(mesh.devices.reshape(4, 8, 4, 4, 2), ("y", "z_lo") + momentum)
    return jax.shard_map(
        per_device,
        mesh=split_mesh,
        in_specs=(P(momentum),) * 3 + (P(),) * 4,
        out_specs=P(("y", "z_lo"), momentum),
        check_vma=False,
    )
```

```python
import jax
import jax.numpy as jnp
from jax import lax
from jax.experimental import pallas as pl
from jax.experimental.pallas import tpu as pltpu
from jax.sharding import Mesh
from jax.sharding import PartitionSpec as P

B = 256
ORB = 12
ATOMS = 21
PAIRS = 128
MODES = 4
MOMENTA = 32
ROWS = 2 * ORB * ORB
HALVES = (ATOMS + 1) // 2

INTERPRET = False


def split(value):
    high = value.astype(jnp.bfloat16)
    low = (value - high.astype(jnp.float32)).astype(jnp.bfloat16)
    return high, low


def split_complex(real, imag):
    real_high, real_low = split(real)
    imag_high, imag_low = split(imag)
    return real_high, real_low, imag_high, imag_low


def left_factors(parts):
    real_high, real_low, imag_high, imag_low = parts
    plain = [real_high, real_high, real_low]
    turned = [imag_high, imag_high, imag_low]
    minus = [-imag_high, -imag_high, -imag_low]
    return (
        jnp.concatenate(plain + minus, axis=1),
        jnp.concatenate(plain + turned, axis=1),
    )


def dot(left, right):
    return lax.dot_general(
        left, right, (((1,), (0,)), ((), ())), preferred_element_type=jnp.float32
    )


def dot_transposed(left, right):
    return lax.dot_general(
        left, right, (((1,), (1,)), ((), ())), preferred_element_type=jnp.float32
    )


def times(left, right_parts, transposed=False):
    for_real, for_imag = left
    real_high, real_low, imag_high, imag_low = right_parts
    axis = 1 if transposed else 0
    product = dot_transposed if transposed else dot
    real_right = jnp.concatenate(
        [real_high, real_low, real_high, imag_high, imag_low, imag_high], axis=axis
    )
    imag_right = jnp.concatenate(
        [imag_high, imag_low, imag_high, real_high, real_low, real_high], axis=axis
    )
    return product(for_real, real_right), product(for_imag, imag_right)


def add(left, right):
    return left[0] + right[0], left[1] + right[1]


def grid_of(axis, shape=(B, B)):
    return lax.broadcasted_iota(jnp.int32, shape, axis)


def inverse_of(system, bare):
    system_real, system_imag = system
    bare_real, bare_imag = bare
    identity = (grid_of(0) == grid_of(1)).astype(jnp.float32)
    diag_real = jnp.sum(bare_real * identity, axis=0, keepdims=True)
    diag_imag = jnp.sum(bare_imag * identity, axis=0, keepdims=True)
    modulus = diag_real * diag_real + diag_imag * diag_imag
    row_real = diag_real / modulus
    row_imag = -diag_imag / modulus
    column_real = jnp.sum(identity * row_real, axis=1, keepdims=True)
    column_imag = jnp.sum(identity * row_imag, axis=1, keepdims=True)
    error_real = identity - (column_real * system_real - column_imag * system_imag)
    error_imag = -(column_real * system_imag + column_imag * system_real)
    plus_real = identity + error_real
    start = (
        plus_real * row_real - error_imag * row_imag,
        plus_real * row_imag + error_imag * row_real,
    )
    error_parts = split_complex(error_real, error_imag)
    squared = times(left_factors(error_parts), error_parts)
    return two_more(squared, start)


def two_more(squared, start):
    squared_parts = split_complex(*squared)
    squared_left = left_factors(squared_parts)
    first = add(start, times(squared_left, split_complex(*start)))
    fourth = times(squared_left, squared_parts)
    fourth_left = left_factors(split_complex(*fourth))
    return add(first, times(fourth_left, split_complex(*first)))


def first_kernel(
    energy_ref, device_ref, lead_ref, coupling_ref, pair_ref, system_ref, green_ref, blocks_ref, rows_ref
):
    energy = energy_ref[0]
    scaled_identity = jnp.where(grid_of(0) == grid_of(1), energy, 0.0)
    lead = (scaled_identity - lead_ref[0, 0], -lead_ref[0, 1])
    green_lead = inverse_of(lead, lead)
    coupling_parts = split_complex(coupling_ref[0, 0], coupling_ref[0, 1])
    half = times(left_factors(coupling_parts), split_complex(*green_lead))
    contact = times(left_factors(split_complex(*half)), coupling_parts, transposed=True)
    bare = (scaled_identity - device_ref[0, 0], -device_ref[0, 1])
    system = (bare[0] - contact[0], bare[1] - contact[1])
    system_ref[0] = system[0]
    system_ref[1] = system[1]
    green = inverse_of(system, bare)
    green_ref[0] = green[0]
    green_ref[1] = green[1]
    take_blocks(green, pair_ref, rows_ref)
    shards, shard_rows = blocks_ref.shape[:2]
    for shard in range(shards):
        blocks_ref[shard] = rows_ref[shard * shard_rows : (shard + 1) * shard_rows, :]


def take_blocks(green, pair_ref, rows_ref):
    real_high, real_low = split(green[0])
    imag_high, imag_low = split(green[1])
    left = jnp.concatenate(
        [
            jnp.concatenate([real_high, real_low], axis=1),
            jnp.concatenate([imag_high, imag_low], axis=1),
        ],
        axis=0,
    )
    row_atom = pair_ref[0:1, :]
    column_atom = pair_ref[1:2, :]
    row_half = row_atom // 2
    row_odd = (row_atom - 2 * row_half) == 1
    row_half = jnp.concatenate([row_half, row_half], axis=1)
    row_odd = jnp.concatenate([row_atom, row_atom], axis=1) - 2 * row_half == 1
    offset = grid_of(0, (B, PAIRS)) - ORB * column_atom
    for first in range(0, ORB, 2):
        pick = jnp.concatenate(
            [(offset == first).astype(jnp.bfloat16), (offset == first + 1).astype(jnp.bfloat16)],
            axis=1,
        )
        columns = dot(left, jnp.concatenate([pick, pick], axis=0))
        for part in range(2):
            found = jnp.zeros((2 * ORB, 2 * PAIRS), jnp.float32)
            for half in range(HALVES):
                begin = part * B + 2 * ORB * half
                if half == HALVES - 1:
                    piece = jnp.concatenate(
                        [columns[begin : begin + 16], jnp.zeros((8, 2 * PAIRS), jnp.float32)], axis=0
                    )
                else:
                    piece = columns[begin : begin + 2 * ORB]
                found = jnp.where(row_half == half, piece, found)
            chosen = jnp.where(row_odd, found[ORB:], found[:ORB])
            for side in range(2):
                row = (part * ORB + first + side) * ORB
                rows_ref[row : row + ORB, :] = chosen[:, side * PAIRS : (side + 1) * PAIRS]


def place_blocks(values, pair_ref):
    row_atom = pair_ref[0:1, :]
    column_atom = pair_ref[1:2, :]
    row_half = row_atom // 2
    row_odd = row_atom - 2 * row_half
    identity = grid_of(0, (PAIRS, PAIRS)) == grid_of(1, (PAIRS, PAIRS))
    column_of = jnp.sum(
        jnp.where(identity, (ORB * column_atom).astype(jnp.float32), 0.0), axis=1, keepdims=True
    ).astype(jnp.int32)
    offset = grid_of(1, (PAIRS, B)) - column_of
    pick = jnp.concatenate(
        [(offset == column).astype(jnp.bfloat16) for column in range(ORB)], axis=0
    )
    results = []
    for part in range(2):
        highs = []
        lows = []
        for column in range(ORB):
            row = (part * ORB + column) * ORB
            block = values[row : row + ORB, :]
            both = jnp.concatenate(
                [jnp.where(row_odd == 0, block, 0.0), jnp.where(row_odd == 1, block, 0.0)], axis=0
            )
            pieces = []
            for half in range(HALVES):
                piece = jnp.where(row_half == half, both, 0.0)
                pieces.append(piece[:16] if half == HALVES - 1 else piece)
            spread = jnp.concatenate(pieces, axis=0)
            high, low = split(spread)
            highs.append(high)
            lows.append(low)
        left = jnp.concatenate(highs + lows, axis=1)
        results.append(dot(left, jnp.concatenate([pick, pick], axis=0)))
    return results


def last_kernel(system_ref, green_ref, blocks_ref, pair_ref, out_ref):
    shards, shard_rows = blocks_ref.shape[:2]
    values = jnp.concatenate([blocks_ref[shard] for shard in range(shards)], axis=0)
    scattering = place_blocks(values, pair_ref)
    second = (system_ref[0] - scattering[0], system_ref[1] - scattering[1])
    green = (green_ref[0], green_ref[1])
    identity = (grid_of(0) == grid_of(1)).astype(jnp.float32)
    product = times(left_factors(split_complex(*green)), split_complex(*second))
    residual = (identity - product[0], -product[1])
    final = two_more(residual, green)
    out_ref[0, 0, 0] = final[0]
    out_ref[0, 0, 1] = final[1]


def vmem(count):
    return [pl.BlockSpec(memory_space=pltpu.VMEM)] * count


def first_call(energy, device_hamiltonian, lead_hamiltonian, lead_coupling, pair_atoms, shards):
    shape = jax.ShapeDtypeStruct((2, B, B), jnp.float32)
    blocks = jax.ShapeDtypeStruct((shards, ROWS // shards, PAIRS), jnp.float32)
    return pl.pallas_call(
        first_kernel,
        out_shape=(shape, shape, blocks),
        in_specs=[pl.BlockSpec(memory_space=pltpu.SMEM)] + vmem(4),
        out_specs=tuple(vmem(3)),
        scratch_shapes=[pltpu.VMEM((ROWS, PAIRS), jnp.float32)],
        name="first_round",
        interpret=INTERPRET,
    )(energy, device_hamiltonian, lead_hamiltonian, lead_coupling, pair_atoms)


def last_call(system, green, blocks, pair_atoms):
    return pl.pallas_call(
        last_kernel,
        out_shape=jax.ShapeDtypeStruct((1, 1, 2, B, B), jnp.float32),
        in_specs=vmem(4),
        out_specs=pl.BlockSpec(memory_space=pltpu.VMEM),
        name="second_round",
        interpret=INTERPRET,
    )(system, green, blocks, pair_atoms)


def exchange(array, axes):
    return lax.all_to_all(array, axes, split_axis=0, concat_axis=0, tiled=True)


def slab_sum_kernel(arrived_ref, out_ref):
    rows = arrived_ref.shape[1]
    groups = out_ref.shape[0] // rows
    members = arrived_ref.shape[0] // groups
    for group in range(groups):
        total = arrived_ref[group * members]
        for member in range(1, members):
            total = total + arrived_ref[group * members + member]
        out_ref[group * rows : (group + 1) * rows, :] = total


def convolve_kernel(lane_ref, shift_ref, occupation_ref, coupling_ref, arrived_ref, out_ref):
    lanes, stacked = arrived_ref.shape[:2]
    rows = out_ref.shape[1]
    planes = stacked // rows
    copies = out_ref.shape[0] // planes
    energies = lanes * planes
    source = lax.broadcasted_iota(jnp.int32, (energies, PAIRS), 0)
    weights = []
    for plane in range(planes):
        target = plane * lanes + lane_ref[0]
        total = jnp.zeros((energies, PAIRS), jnp.float32)
        for mode in range(MODES):
            occupied = occupation_ref[mode]
            shift = shift_ref[mode]
            factor = jnp.where(source == target - shift, occupied, 0.0) + jnp.where(
                source == target + shift, occupied + 1.0, 0.0
            )
            total = total + factor * coupling_ref[mode : mode + 1, :]
        weights.append(total / MOMENTA)
    results = [jnp.zeros((rows, PAIRS), jnp.float32) for _ in range(planes)]
    for lane in range(lanes):
        for plane in range(planes):
            piece = arrived_ref[lane, plane * rows : (plane + 1) * rows, :]
            energy = plane * lanes + lane
            for target in range(planes):
                results[target] = results[target] + weights[target][energy : energy + 1, :] * piece
    for plane in range(planes):
        for copy in range(copies):
            out_ref[plane * copies + copy] = results[plane]


def per_device(
    device_hamiltonian,
    lead_hamiltonian,
    lead_coupling,
    pair_atoms,
    phonon_shift,
    occupation,
    phonon_coupling,
):
    planes = lax.axis_size("y")
    lanes = lax.axis_size("z_lo")
    slab = planes * lax.axis_size("x") * lax.axis_size("core")
    rows = ROWS // slab
    energy_index = lax.axis_index(("y", "z_lo"))
    energy = -1.0 + 2.0 * (energy_index.astype(jnp.float32) + 0.5) / (planes * lanes)
    system, green, blocks = first_call(
        energy[None], device_hamiltonian, lead_hamiltonian, lead_coupling, pair_atoms, slab
    )
    arrived = exchange(blocks, ("y", "x", "core"))
    summed = pl.pallas_call(
        slab_sum_kernel,
        out_shape=jax.ShapeDtypeStruct((planes * rows, PAIRS), jnp.float32),
        in_specs=vmem(1),
        out_specs=vmem(1)[0],
        name="slab_sum",
        interpret=INTERPRET,
    )(arrived)
    near = lax.ppermute(summed, "z_hi", [(0, 1), (1, 0), (2, 3), (3, 2)])
    paired = summed + near
    far = lax.ppermute(paired, "z_hi", [(0, 3), (3, 0), (1, 2), (2, 1)])
    copies = jnp.broadcast_to(paired + far, (lanes, planes * rows, PAIRS))
    arrived = exchange(copies, "z_lo")
    self_energy = pl.pallas_call(
        convolve_kernel,
        out_shape=jax.ShapeDtypeStruct((slab, rows, PAIRS), jnp.float32),
        in_specs=[pl.BlockSpec(memory_space=pltpu.SMEM)] * 3 + vmem(2),
        out_specs=vmem(1)[0],
        name="phonon_sum",
        interpret=INTERPRET,
    )(lax.axis_index("z_lo")[None], phonon_shift, occupation, phonon_coupling, arrived)
    arrived = exchange(self_energy, ("y", "x", "core"))
    return last_call(system, green, arrived, pair_atoms)


def solution(mesh):
    momentum = ("x", "z_hi", "core")
    split_mesh = Mesh(mesh.devices.reshape(4, 8, 4, 4, 2), ("y", "z_lo") + momentum)
    return jax.shard_map(
        per_device,
        mesh=split_mesh,
        in_specs=(P(momentum),) * 3 + (P(),) * 4,
        out_specs=P(("y", "z_lo"), momentum),
        check_vma=False,
    )
```

```python
import jax
import jax.numpy as jnp
from jax import lax
from jax.experimental import pallas as pl
from jax.experimental.pallas import tpu as pltpu
from jax.sharding import Mesh
from jax.sharding import PartitionSpec as P

B = 256
ORB = 12
ATOMS = 21
PAIRS = 128
MODES = 4
MOMENTA = 32
PLANES = 4
LANES = 8
SHARE = PAIRS // LANES
ROWS = 2 * ORB * ORB
HALVES = (ATOMS + 1) // 2

INTERPRET = False


def split(value):
    high = value.astype(jnp.bfloat16)
    low = (value - high.astype(jnp.float32)).astype(jnp.bfloat16)
    return high, low


def split_complex(real, imag):
    real_high, real_low = split(real)
    imag_high, imag_low = split(imag)
    return real_high, real_low, imag_high, imag_low


def left_factors(parts):
    real_high, real_low, imag_high, imag_low = parts
    plain = [real_high, real_high, real_low]
    turned = [imag_high, imag_high, imag_low]
    minus = [-imag_high, -imag_high, -imag_low]
    return (
        jnp.concatenate(plain + minus, axis=1),
        jnp.concatenate(plain + turned, axis=1),
    )


def dot(left, right):
    return lax.dot_general(
        left, right, (((1,), (0,)), ((), ())), preferred_element_type=jnp.float32
    )


def dot_transposed(left, right):
    return lax.dot_general(
        left, right, (((1,), (1,)), ((), ())), preferred_element_type=jnp.float32
    )


def times(left, right_parts, transposed=False):
    for_real, for_imag = left
    real_high, real_low, imag_high, imag_low = right_parts
    axis = 1 if transposed else 0
    product = dot_transposed if transposed else dot
    real_right = jnp.concatenate(
        [real_high, real_low, real_high, imag_high, imag_low, imag_high], axis=axis
    )
    imag_right = jnp.concatenate(
        [imag_high, imag_low, imag_high, real_high, real_low, real_high], axis=axis
    )
    return product(for_real, real_right), product(for_imag, imag_right)


def add(left, right):
    return left[0] + right[0], left[1] + right[1]


def grid_of(axis, shape=(B, B)):
    return lax.broadcasted_iota(jnp.int32, shape, axis)


def inverse_of(system, bare):
    system_real, system_imag = system
    bare_real, bare_imag = bare
    identity = (grid_of(0) == grid_of(1)).astype(jnp.float32)
    diag_real = jnp.sum(bare_real * identity, axis=0, keepdims=True)
    diag_imag = jnp.sum(bare_imag * identity, axis=0, keepdims=True)
    modulus = diag_real * diag_real + diag_imag * diag_imag
    row_real = diag_real / modulus
    row_imag = -diag_imag / modulus
    column_real = jnp.sum(identity * row_real, axis=1, keepdims=True)
    column_imag = jnp.sum(identity * row_imag, axis=1, keepdims=True)
    error_real = identity - (column_real * system_real - column_imag * system_imag)
    error_imag = -(column_real * system_imag + column_imag * system_real)
    plus_real = identity + error_real
    start = (
        plus_real * row_real - error_imag * row_imag,
        plus_real * row_imag + error_imag * row_real,
    )
    error_parts = split_complex(error_real, error_imag)
    squared = times(left_factors(error_parts), error_parts)
    return two_more(squared, start)


def two_more(squared, start):
    squared_parts = split_complex(*squared)
    squared_left = left_factors(squared_parts)
    first = add(start, times(squared_left, split_complex(*start)))
    fourth = times(squared_left, squared_parts)
    fourth_left = left_factors(split_complex(*fourth))
    return add(first, times(fourth_left, split_complex(*first)))


def first_kernel(
    energy_ref, device_ref, lead_ref, coupling_ref, pair_ref, system_ref, green_ref, blocks_ref, rows_ref
):
    energy = energy_ref[0]
    scaled_identity = jnp.where(grid_of(0) == grid_of(1), energy, 0.0)
    lead = (scaled_identity - lead_ref[0, 0], -lead_ref[0, 1])
    green_lead = inverse_of(lead, lead)
    coupling_parts = split_complex(coupling_ref[0, 0], coupling_ref[0, 1])
    half = times(left_factors(coupling_parts), split_complex(*green_lead))
    contact = times(left_factors(split_complex(*half)), coupling_parts, transposed=True)
    bare = (scaled_identity - device_ref[0, 0], -device_ref[0, 1])
    system = (bare[0] - contact[0], bare[1] - contact[1])
    system_ref[0] = system[0]
    system_ref[1] = system[1]
    green = inverse_of(system, bare)
    green_ref[0] = green[0]
    green_ref[1] = green[1]
    take_blocks(green, pair_ref, rows_ref)
    shards = blocks_ref.shape[0]
    shard_rows = ROWS // shards
    for row in range(ROWS):
        place = (row % shard_rows) * PAIRS
        blocks_ref[row // shard_rows, :, place : place + PAIRS] = rows_ref[row : row + 1, :]


def take_blocks(green, pair_ref, rows_ref):
    real_high, real_low = split(green[0])
    imag_high, imag_low = split(green[1])
    left = jnp.concatenate(
        [
            jnp.concatenate([real_high, real_low], axis=1),
            jnp.concatenate([imag_high, imag_low], axis=1),
        ],
        axis=0,
    )
    row_atom = pair_ref[0:1, :]
    column_atom = pair_ref[1:2, :]
    row_half = row_atom // 2
    row_odd = (row_atom - 2 * row_half) == 1
    row_half = jnp.concatenate([row_half, row_half], axis=1)
    row_odd = jnp.concatenate([row_atom, row_atom], axis=1) - 2 * row_half == 1
    offset = grid_of(0, (B, PAIRS)) - ORB * column_atom
    for first in range(0, ORB, 2):
        pick = jnp.concatenate(
            [(offset == first).astype(jnp.bfloat16), (offset == first + 1).astype(jnp.bfloat16)],
            axis=1,
        )
        columns = dot(left, jnp.concatenate([pick, pick], axis=0))
        for part in range(2):
            found = jnp.zeros((2 * ORB, 2 * PAIRS), jnp.float32)
            for half in range(HALVES):
                begin = part * B + 2 * ORB * half
                if half == HALVES - 1:
                    piece = jnp.concatenate(
                        [columns[begin : begin + 16], jnp.zeros((8, 2 * PAIRS), jnp.float32)], axis=0
                    )
                else:
                    piece = columns[begin : begin + 2 * ORB]
                found = jnp.where(row_half == half, piece, found)
            chosen = jnp.where(row_odd, found[ORB:], found[:ORB])
            for side in range(2):
                row = (part * ORB + first + side) * ORB
                rows_ref[row : row + ORB, :] = chosen[:, side * PAIRS : (side + 1) * PAIRS]


def place_blocks(values, pair_ref):
    row_atom = pair_ref[0:1, :]
    column_atom = pair_ref[1:2, :]
    row_half = row_atom // 2
    row_odd = row_atom - 2 * row_half
    identity = grid_of(0, (PAIRS, PAIRS)) == grid_of(1, (PAIRS, PAIRS))
    column_of = jnp.sum(
        jnp.where(identity, (ORB * column_atom).astype(jnp.float32), 0.0), axis=1, keepdims=True
    ).astype(jnp.int32)
    offset = grid_of(1, (PAIRS, B)) - column_of
    pick = jnp.concatenate(
        [(offset == column).astype(jnp.bfloat16) for column in range(ORB)], axis=0
    )
    results = []
    for part in range(2):
        highs = []
        lows = []
        for column in range(ORB):
            row = (part * ORB + column) * ORB
            block = values[row : row + ORB, :]
            both = jnp.concatenate(
                [jnp.where(row_odd == 0, block, 0.0), jnp.where(row_odd == 1, block, 0.0)], axis=0
            )
            pieces = []
            for half in range(HALVES):
                piece = jnp.where(row_half == half, both, 0.0)
                pieces.append(piece[:16] if half == HALVES - 1 else piece)
            spread = jnp.concatenate(pieces, axis=0)
            high, low = split(spread)
            highs.append(high)
            lows.append(low)
        left = jnp.concatenate(highs + lows, axis=1)
        results.append(dot(left, jnp.concatenate([pick, pick], axis=0)))
    return results


def last_kernel(system_ref, green_ref, blocks_ref, pair_ref, out_ref, rows_ref):
    shard_rows = ROWS // blocks_ref.shape[0]
    for row in range(ROWS):
        place = (row % shard_rows) * PAIRS
        rows_ref[row : row + 1, :] = blocks_ref[row // shard_rows, :, place : place + PAIRS]
    scattering = place_blocks(rows_ref, pair_ref)
    second = (system_ref[0] - scattering[0], system_ref[1] - scattering[1])
    green = (green_ref[0], green_ref[1])
    identity = (grid_of(0) == grid_of(1)).astype(jnp.float32)
    product = times(left_factors(split_complex(*green)), split_complex(*second))
    residual = (identity - product[0], -product[1])
    final = two_more(residual, green)
    out_ref[0, 0, 0] = final[0]
    out_ref[0, 0, 1] = final[1]


def vmem(count):
    return [pl.BlockSpec(memory_space=pltpu.VMEM)] * count


def first_call(energy, device_hamiltonian, lead_hamiltonian, lead_coupling, pair_atoms, shards):
    shape = jax.ShapeDtypeStruct((2, B, B), jnp.float32)
    blocks = jax.ShapeDtypeStruct((shards, 1, ROWS // shards * PAIRS), jnp.float32)
    return pl.pallas_call(
        first_kernel,
        out_shape=(shape, shape, blocks),
        in_specs=[pl.BlockSpec(memory_space=pltpu.SMEM)] + vmem(4),
        out_specs=tuple(vmem(3)),
        scratch_shapes=[pltpu.VMEM((ROWS, PAIRS), jnp.float32)],
        name="first_round",
        interpret=INTERPRET,
    )(energy, device_hamiltonian, lead_hamiltonian, lead_coupling, pair_atoms)


def last_call(system, green, blocks, pair_atoms):
    return pl.pallas_call(
        last_kernel,
        out_shape=jax.ShapeDtypeStruct((1, 1, 2, B, B), jnp.float32),
        in_specs=vmem(4),
        out_specs=pl.BlockSpec(memory_space=pltpu.VMEM),
        scratch_shapes=[pltpu.VMEM((ROWS, PAIRS), jnp.float32)],
        name="second_round",
        interpret=INTERPRET,
    )(system, green, blocks, pair_atoms)


def exchange(array, axes):
    return lax.all_to_all(array, axes, split_axis=0, concat_axis=0, tiled=True)


def lanes_of(width=PAIRS):
    return lax.broadcasted_iota(jnp.int32, (1, width), 1)


def slab_sum_kernel(arrived_ref, out_ref):
    members = arrived_ref.shape[0] // PLANES
    totals = []
    for plane in range(PLANES):
        total = arrived_ref[plane * members]
        for member in range(1, members):
            total = total + arrived_ref[plane * members + member]
        totals.append(total)
    own = lanes_of() // SHARE
    for lane in range(LANES):
        begin = lane * PAIRS
        shared = jnp.zeros((1, PAIRS), jnp.float32)
        for plane in range(PLANES):
            tail = jnp.where(own == lane, totals[plane][:, LANES * PAIRS :], 0.0)
            shared = shared + pltpu.roll(tail, (SHARE * (plane - lane)) % PAIRS, 1)
        for column in range(out_ref.shape[0] // LANES):
            piece = column * LANES + lane
            for plane in range(PLANES):
                out_ref[piece, :, plane * PAIRS : (plane + 1) * PAIRS] = totals[plane][
                    :, begin : begin + PAIRS
                ]
            out_ref[piece, :, PLANES * PAIRS :] = shared


def convolve_kernel(
    lane_ref, shift_ref, occupation_ref, coupling_ref, arrived_ref, out_ref, sums_ref, tails_ref
):
    energies = PLANES * LANES
    for lane in range(LANES):
        total = arrived_ref[lane]
        for column in range(1, arrived_ref.shape[0] // LANES):
            total = total + arrived_ref[column * LANES + lane]
        for plane in range(PLANES):
            energy = plane * LANES + lane
            sums_ref[energy : energy + 1, :PAIRS] = total[:, plane * PAIRS : (plane + 1) * PAIRS]
        tails_ref[lane : lane + 1, :] = total[:, PLANES * PAIRS :]
    kept = lanes_of() < SHARE
    tails = tails_ref[...]
    for plane in range(PLANES):
        moved = pltpu.roll(tails, (-SHARE * plane) % PAIRS, 1)
        sums_ref[plane * LANES : (plane + 1) * LANES, PAIRS:] = jnp.where(kept, moved, 0.0)
    target = lax.broadcasted_iota(jnp.int32, (energies, energies), 0)
    source = lax.broadcasted_iota(jnp.int32, (energies, energies), 1)
    factors = []
    for mode in range(MODES):
        occupied = occupation_ref[mode] / MOMENTA
        more = (occupation_ref[mode] + 1.0) / MOMENTA
        shift = shift_ref[mode]
        factors.append(
            jnp.where(source == target - shift, occupied, 0.0)
            + jnp.where(source == target + shift, more, 0.0)
        )
    shifted = lax.dot_general(
        jnp.concatenate(factors, axis=0),
        sums_ref[...],
        (((1,), (0,)), ((), ())),
        precision=lax.Precision.HIGHEST,
        preferred_element_type=jnp.float32,
    )
    coupling = coupling_ref[...]
    own_coupling = pltpu.roll(coupling, (PAIRS - SHARE * lane_ref[0]) % PAIRS, 1)
    both = jnp.concatenate([coupling, own_coupling], axis=1)
    result = jnp.zeros((energies, 2 * PAIRS), jnp.float32)
    for mode in range(MODES):
        result = result + shifted[mode * energies : (mode + 1) * energies] * both[mode : mode + 1]
    tails = jnp.zeros((LANES, PAIRS), jnp.float32)
    for plane in range(PLANES):
        piece = jnp.where(kept, result[plane * LANES : (plane + 1) * LANES, PAIRS:], 0.0)
        tails = tails + pltpu.roll(piece, SHARE * plane, 1)
    for lane in range(LANES):
        for plane in range(PLANES):
            energy = plane * LANES + lane
            out_ref[lane, :, plane * PAIRS : (plane + 1) * PAIRS] = result[
                energy : energy + 1, :PAIRS
            ]
        out_ref[lane, :, PLANES * PAIRS :] = tails[lane : lane + 1]


def spread_kernel(arrived_ref, out_ref):
    copies = out_ref.shape[0] // PLANES
    own = lanes_of() // SHARE
    for plane in range(PLANES):
        pieces = []
        shared = jnp.zeros((1, PAIRS), jnp.float32)
        for lane in range(LANES):
            pieces.append(arrived_ref[lane, :, plane * PAIRS : (plane + 1) * PAIRS])
            tail = jnp.where(own == plane, arrived_ref[lane, :, PLANES * PAIRS :], 0.0)
            shared = shared + pltpu.roll(tail, (SHARE * (lane - plane)) % PAIRS, 1)
        whole = jnp.concatenate(pieces + [shared], axis=1)
        for copy in range(copies):
            out_ref[plane * copies + copy] = whole


def kernel_call(kernel, name, shape, *arguments, scalars=0, scratch=()):
    return pl.pallas_call(
        kernel,
        out_shape=jax.ShapeDtypeStruct(shape, jnp.float32),
        in_specs=[pl.BlockSpec(memory_space=pltpu.SMEM)] * scalars
        + vmem(len(arguments) - scalars),
        out_specs=vmem(1)[0],
        scratch_shapes=[pltpu.VMEM(extent, jnp.float32) for extent in scratch],
        name=name,
        interpret=INTERPRET,
    )(*arguments)


def per_device(
    device_hamiltonian,
    lead_hamiltonian,
    lead_coupling,
    pair_atoms,
    phonon_shift,
    occupation,
    phonon_coupling,
):
    slab = PLANES * lax.axis_size("x") * lax.axis_size("core")
    width = PLANES * PAIRS + PAIRS
    energy_index = lax.axis_index(("y", "z_lo"))
    energy = -1.0 + 2.0 * (energy_index.astype(jnp.float32) + 0.5) / (PLANES * LANES)
    system, green, blocks = first_call(
        energy[None], device_hamiltonian, lead_hamiltonian, lead_coupling, pair_atoms, slab
    )
    arrived = exchange(blocks, ("y", "x", "core"))
    columns = lax.axis_size("z_hi")
    summed = kernel_call(slab_sum_kernel, "slab_sum", (columns * LANES, 1, width), arrived)
    arrived = exchange(summed, ("z_hi", "z_lo"))
    shifted = kernel_call(
        convolve_kernel,
        "phonon_sum",
        (LANES, 1, width),
        lax.axis_index("z_lo")[None],
        phonon_shift,
        occupation,
        phonon_coupling,
        arrived,
        scalars=3,
        scratch=((PLANES * LANES, 2 * PAIRS), (LANES, PAIRS)),
    )
    arrived = exchange(shifted, "z_lo")
    spread = kernel_call(spread_kernel, "spread", blocks.shape, arrived)
    arrived = exchange(spread, ("y", "x", "core"))
    return last_call(system, green, arrived, pair_atoms)


def solution(mesh):
    momentum = ("x", "z_hi", "core")
    split_mesh = Mesh(mesh.devices.reshape(PLANES, LANES, 4, 4, 2), ("y", "z_lo") + momentum)
    return jax.shard_map(
        per_device,
        mesh=split_mesh,
        in_specs=(P(momentum),) * 3 + (P(),) * 4,
        out_specs=P(("y", "z_lo"), momentum),
        check_vma=False,
    )
```

```python
import jax
import jax.numpy as jnp
from jax import lax
from jax.experimental import pallas as pl
from jax.experimental.pallas import tpu as pltpu
from jax.sharding import Mesh
from jax.sharding import PartitionSpec as P

B = 256
ORB = 12
ATOMS = 21
PAIRS = 128
MODES = 4
MOMENTA = 32
PLANES = 4
LANES = 8
ROWS = 2 * ORB * ORB
HALVES = (ATOMS + 1) // 2

INTERPRET = False


def split(value):
    high = value.astype(jnp.bfloat16)
    low = (value - high.astype(jnp.float32)).astype(jnp.bfloat16)
    return high, low


def split_complex(real, imag):
    real_high, real_low = split(real)
    imag_high, imag_low = split(imag)
    return real_high, real_low, imag_high, imag_low


def left_factors(parts):
    real_high, real_low, imag_high, imag_low = parts
    plain = [real_high, real_high, real_low]
    turned = [imag_high, imag_high, imag_low]
    minus = [-imag_high, -imag_high, -imag_low]
    return (
        jnp.concatenate(plain + minus, axis=1),
        jnp.concatenate(plain + turned, axis=1),
    )


def dot(left, right):
    return lax.dot_general(
        left, right, (((1,), (0,)), ((), ())), preferred_element_type=jnp.float32
    )


def dot_transposed(left, right):
    return lax.dot_general(
        left, right, (((1,), (1,)), ((), ())), preferred_element_type=jnp.float32
    )


def times(left, right_parts, transposed=False):
    for_real, for_imag = left
    real_high, real_low, imag_high, imag_low = right_parts
    axis = 1 if transposed else 0
    product = dot_transposed if transposed else dot
    real_right = jnp.concatenate(
        [real_high, real_low, real_high, imag_high, imag_low, imag_high], axis=axis
    )
    imag_right = jnp.concatenate(
        [imag_high, imag_low, imag_high, real_high, real_low, real_high], axis=axis
    )
    return product(for_real, real_right), product(for_imag, imag_right)


def add(left, right):
    return left[0] + right[0], left[1] + right[1]


def grid_of(axis, shape=(B, B)):
    return lax.broadcasted_iota(jnp.int32, shape, axis)


def error_and_start(system, bare):
    system_real, system_imag = system
    bare_real, bare_imag = bare
    identity = (grid_of(0) == grid_of(1)).astype(jnp.float32)
    diag_real = jnp.sum(bare_real * identity, axis=0, keepdims=True)
    diag_imag = jnp.sum(bare_imag * identity, axis=0, keepdims=True)
    modulus = diag_real * diag_real + diag_imag * diag_imag
    row_real = diag_real / modulus
    row_imag = -diag_imag / modulus
    column_real = jnp.sum(identity * row_real, axis=1, keepdims=True)
    column_imag = jnp.sum(identity * row_imag, axis=1, keepdims=True)
    error_real = identity - (column_real * system_real - column_imag * system_imag)
    error_imag = -(column_real * system_imag + column_imag * system_real)
    plus_real = identity + error_real
    start = (
        plus_real * row_real - error_imag * row_imag,
        plus_real * row_imag + error_imag * row_real,
    )
    return (error_real, error_imag), start


def inverse_of(system, bare):
    error, start = error_and_start(system, bare)
    error_parts = split_complex(*error)
    squared = times(left_factors(error_parts), error_parts)
    return two_more(squared, start)


def two_more(squared, start):
    squared_parts = split_complex(*squared)
    squared_left = left_factors(squared_parts)
    first = add(start, times(squared_left, split_complex(*start)))
    fourth = times(squared_left, squared_parts)
    fourth_left = left_factors(split_complex(*fourth))
    return add(first, times(fourth_left, split_complex(*first)))


def contact_of(system, coupling):
    error, start = error_and_start(system, system)
    error_parts = split_complex(*error)
    coupling_parts = split_complex(*coupling)
    right = times(left_factors(split_complex(*start)), coupling_parts, transposed=True)
    squared_parts = split_complex(*times(left_factors(error_parts), error_parts))
    fourth = times(left_factors(squared_parts), squared_parts)
    left = add(coupling, times(left_factors(coupling_parts), squared_parts))
    left = add(left, times(left_factors(split_complex(*left)), split_complex(*fourth)))
    return times(left_factors(split_complex(*left)), split_complex(*right))


def first_kernel(
    energy_ref,
    device_hbm,
    lead_hbm,
    coupling_hbm,
    pair_ref,
    system_ref,
    green_ref,
    blocks_ref,
    rows_ref,
    device_ref,
    lead_ref,
    coupling_ref,
    semaphores,
):
    lead_copy = pltpu.make_async_copy(lead_hbm.at[0], lead_ref, semaphores.at[0])
    coupling_copy = pltpu.make_async_copy(coupling_hbm.at[0], coupling_ref, semaphores.at[1])
    device_copy = pltpu.make_async_copy(device_hbm.at[0], device_ref, semaphores.at[2])
    lead_copy.start()
    coupling_copy.start()
    device_copy.start()
    energy = energy_ref[0]
    scaled_identity = jnp.where(grid_of(0) == grid_of(1), energy, 0.0)
    lead_copy.wait()
    coupling_copy.wait()
    lead = (scaled_identity - lead_ref[0], -lead_ref[1])
    contact = contact_of(lead, (coupling_ref[0], coupling_ref[1]))
    device_copy.wait()
    bare = (scaled_identity - device_ref[0], -device_ref[1])
    system = (bare[0] - contact[0], bare[1] - contact[1])
    system_ref[0] = system[0]
    system_ref[1] = system[1]
    green = inverse_of(system, bare)
    green_ref[0] = green[0]
    green_ref[1] = green[1]
    take_blocks(green, pair_ref, rows_ref)
    shards = blocks_ref.shape[0]
    shard_rows = ROWS // shards
    for row in range(ROWS):
        place = (row % shard_rows) * PAIRS
        blocks_ref[row // shard_rows, :, place : place + PAIRS] = rows_ref[row : row + 1, :]


def take_blocks(green, pair_ref, rows_ref):
    real_high, real_low = split(green[0])
    imag_high, imag_low = split(green[1])
    left = jnp.concatenate(
        [
            jnp.concatenate([real_high, real_low], axis=1),
            jnp.concatenate([imag_high, imag_low], axis=1),
        ],
        axis=0,
    )
    row_atom = pair_ref[0:1, :]
    column_atom = pair_ref[1:2, :]
    row_half = row_atom // 2
    row_odd = (row_atom - 2 * row_half) == 1
    row_half = jnp.concatenate([row_half, row_half], axis=1)
    row_odd = jnp.concatenate([row_atom, row_atom], axis=1) - 2 * row_half == 1
    offset = grid_of(0, (B, PAIRS)) - ORB * column_atom
    for first in range(0, ORB, 2):
        pick = jnp.concatenate(
            [(offset == first).astype(jnp.bfloat16), (offset == first + 1).astype(jnp.bfloat16)],
            axis=1,
        )
        columns = dot(left, jnp.concatenate([pick, pick], axis=0))
        for part in range(2):
            found = jnp.zeros((2 * ORB, 2 * PAIRS), jnp.float32)
            for half in range(HALVES):
                begin = part * B + 2 * ORB * half
                if half == HALVES - 1:
                    piece = jnp.concatenate(
                        [columns[begin : begin + 16], jnp.zeros((8, 2 * PAIRS), jnp.float32)], axis=0
                    )
                else:
                    piece = columns[begin : begin + 2 * ORB]
                found = jnp.where(row_half == half, piece, found)
            chosen = jnp.where(row_odd, found[ORB:], found[:ORB])
            for side in range(2):
                row = (part * ORB + first + side) * ORB
                rows_ref[row : row + ORB, :] = chosen[:, side * PAIRS : (side + 1) * PAIRS]


def place_blocks(values, pair_ref):
    row_atom = pair_ref[0:1, :]
    column_atom = pair_ref[1:2, :]
    row_half = row_atom // 2
    row_odd = row_atom - 2 * row_half
    identity = grid_of(0, (PAIRS, PAIRS)) == grid_of(1, (PAIRS, PAIRS))
    column_of = jnp.sum(
        jnp.where(identity, (ORB * column_atom).astype(jnp.float32), 0.0), axis=1, keepdims=True
    ).astype(jnp.int32)
    offset = grid_of(1, (PAIRS, B)) - column_of
    pick = jnp.concatenate(
        [(offset == column).astype(jnp.bfloat16) for column in range(ORB)], axis=0
    )
    results = []
    for part in range(2):
        highs = []
        lows = []
        for column in range(ORB):
            row = (part * ORB + column) * ORB
            block = values[row : row + ORB, :]
            both = jnp.concatenate(
                [jnp.where(row_odd == 0, block, 0.0), jnp.where(row_odd == 1, block, 0.0)], axis=0
            )
            pieces = []
            for half in range(HALVES):
                piece = jnp.where(row_half == half, both, 0.0)
                pieces.append(piece[:16] if half == HALVES - 1 else piece)
            spread = jnp.concatenate(pieces, axis=0)
            high, low = split(spread)
            highs.append(high)
            lows.append(low)
        left = jnp.concatenate(highs + lows, axis=1)
        results.append(dot(left, jnp.concatenate([pick, pick], axis=0)))
    return results


def last_kernel(system_ref, green_ref, blocks_ref, pair_ref, out_ref, rows_ref):
    shard_rows = ROWS // blocks_ref.shape[0]
    for row in range(ROWS):
        place = (row % shard_rows) * PAIRS
        rows_ref[row : row + 1, :] = blocks_ref[row // shard_rows, :, place : place + PAIRS]
    scattering = place_blocks(rows_ref, pair_ref)
    second = (system_ref[0] - scattering[0], system_ref[1] - scattering[1])
    green = (green_ref[0], green_ref[1])
    identity = (grid_of(0) == grid_of(1)).astype(jnp.float32)
    product = times(left_factors(split_complex(*green)), split_complex(*second))
    residual = (identity - product[0], -product[1])
    final = two_more(residual, green)
    out_ref[0, 0, 0] = final[0]
    out_ref[0, 0, 1] = final[1]


def vmem(count):
    return [pl.BlockSpec(memory_space=pltpu.VMEM)] * count


def near_core(array):
    return array if INTERPRET else pltpu.with_memory_space_constraint(array, pltpu.VMEM)


def near_shape(*shape):
    return jax.ShapeDtypeStruct(shape, jnp.float32) if INTERPRET else pltpu.VMEM(shape, jnp.float32)


def first_call(energy, device_hamiltonian, lead_hamiltonian, lead_coupling, pair_atoms, shards):
    shape = near_shape(2, B, B)
    blocks = near_shape(shards, 1, ROWS // shards * PAIRS)
    return pl.pallas_call(
        first_kernel,
        out_shape=(shape, shape, blocks),
        in_specs=[pl.BlockSpec(memory_space=pltpu.SMEM)]
        + [pl.BlockSpec(memory_space=pl.ANY)] * 3
        + vmem(1),
        out_specs=tuple(vmem(3)),
        scratch_shapes=[pltpu.VMEM((ROWS, PAIRS), jnp.float32)]
        + [pltpu.VMEM((2, B, B), jnp.float32)] * 3
        + [pltpu.SemaphoreType.DMA((3,))],
        name="first_round",
        interpret=INTERPRET,
    )(energy, device_hamiltonian, lead_hamiltonian, lead_coupling, pair_atoms)


def last_call(system, green, blocks, pair_atoms):
    return pl.pallas_call(
        last_kernel,
        out_shape=jax.ShapeDtypeStruct((1, 1, 2, B, B), jnp.float32),
        in_specs=vmem(4),
        out_specs=pl.BlockSpec(memory_space=pltpu.VMEM),
        scratch_shapes=[pltpu.VMEM((ROWS, PAIRS), jnp.float32)],
        name="second_round",
        interpret=INTERPRET,
    )(near_core(system), near_core(green), near_core(blocks), pair_atoms)


def exchange(array, axes):
    return lax.all_to_all(array, axes, split_axis=0, concat_axis=0, tiled=True)


def slab_sum_kernel(arrived_ref, out_ref):
    members = arrived_ref.shape[0] // PLANES
    rows = out_ref.shape[0] // PLANES
    for plane in range(PLANES):
        total = arrived_ref[plane * members]
        for member in range(1, members):
            total = total + arrived_ref[plane * members + member]
        for row in range(rows):
            place = plane * rows + row
            out_ref[place : place + 1, :] = total[:, row * PAIRS : (row + 1) * PAIRS]


def pair_kernel(own_ref, arrived_ref, out_ref):
    out_ref[...] = own_ref[...] + arrived_ref[...]


def copies_kernel(own_ref, arrived_ref, out_ref):
    total = own_ref[...] + arrived_ref[...]
    for copy in range(out_ref.shape[0]):
        out_ref[copy] = total


def convolve_kernel(lane_ref, shift_ref, occupation_ref, coupling_ref, arrived_ref, out_ref):
    lanes, stacked = arrived_ref.shape[:2]
    planes = PLANES
    rows = stacked // planes
    copies = out_ref.shape[0] // planes
    energies = lanes * planes
    source = lax.broadcasted_iota(jnp.int32, (energies, PAIRS), 0)
    weights = []
    for plane in range(planes):
        target = plane * lanes + lane_ref[0]
        total = jnp.zeros((energies, PAIRS), jnp.float32)
        for mode in range(MODES):
            occupied = occupation_ref[mode]
            shift = shift_ref[mode]
            factor = jnp.where(source == target - shift, occupied, 0.0) + jnp.where(
                source == target + shift, occupied + 1.0, 0.0
            )
            total = total + factor * coupling_ref[mode : mode + 1, :]
        weights.append(total / MOMENTA)
    results = [jnp.zeros((rows, PAIRS), jnp.float32) for _ in range(planes)]
    for lane in range(lanes):
        for plane in range(planes):
            piece = arrived_ref[lane, plane * rows : (plane + 1) * rows, :]
            energy = plane * lanes + lane
            for target in range(planes):
                results[target] = results[target] + weights[target][energy : energy + 1, :] * piece
    for plane in range(planes):
        for row in range(rows):
            for copy in range(copies):
                out_ref[plane * copies + copy, :, row * PAIRS : (row + 1) * PAIRS] = results[plane][
                    row : row + 1
                ]


def kernel_call(kernel, name, shape, *arguments, scalars=0, scratch=()):
    arguments = arguments[:scalars] + tuple(
        near_core(argument) for argument in arguments[scalars:]
    )
    return pl.pallas_call(
        kernel,
        out_shape=near_shape(*shape),
        in_specs=[pl.BlockSpec(memory_space=pltpu.SMEM)] * scalars
        + vmem(len(arguments) - scalars),
        out_specs=vmem(1)[0],
        scratch_shapes=[pltpu.VMEM(extent, jnp.float32) for extent in scratch],
        name=name,
        interpret=INTERPRET,
    )(*arguments)


def per_device(
    device_hamiltonian,
    lead_hamiltonian,
    lead_coupling,
    pair_atoms,
    phonon_shift,
    occupation,
    phonon_coupling,
):
    slab = PLANES * lax.axis_size("x") * lax.axis_size("core")
    energy_index = lax.axis_index(("y", "z_lo"))
    energy = -1.0 + 2.0 * (energy_index.astype(jnp.float32) + 0.5) / (PLANES * LANES)
    system, green, blocks = first_call(
        energy[None], device_hamiltonian, lead_hamiltonian, lead_coupling, pair_atoms, slab
    )
    arrived = exchange(blocks, ("y", "x", "core"))
    rows = PLANES * ROWS // slab
    summed = kernel_call(slab_sum_kernel, "slab_sum", (rows, PAIRS), arrived)
    near = lax.ppermute(summed, "z_hi", [(0, 1), (1, 0), (2, 3), (3, 2)])
    paired = kernel_call(pair_kernel, "pair_sum", (rows, PAIRS), summed, near)
    far = lax.ppermute(paired, "z_hi", [(0, 3), (3, 0), (1, 2), (2, 1)])
    copies = kernel_call(copies_kernel, "column_sum", (LANES, rows, PAIRS), paired, far)
    arrived = exchange(copies, "z_lo")
    spread = kernel_call(
        convolve_kernel,
        "phonon_sum",
        blocks.shape,
        lax.axis_index("z_lo")[None],
        phonon_shift,
        occupation,
        phonon_coupling,
        arrived,
        scalars=3,
    )
    arrived = exchange(spread, ("y", "x", "core"))
    return last_call(system, green, arrived, pair_atoms)


def solution(mesh):
    momentum = ("x", "z_hi", "core")
    split_mesh = Mesh(mesh.devices.reshape(PLANES, LANES, 4, 4, 2), ("y", "z_lo") + momentum)
    return jax.shard_map(
        per_device,
        mesh=split_mesh,
        in_specs=(P(momentum),) * 3 + (P(),) * 4,
        out_specs=P(("y", "z_lo"), momentum),
        check_vma=False,
    )
```

```python
import jax
import jax.numpy as jnp
from jax import lax
from jax.experimental import pallas as pl
from jax.experimental.pallas import tpu as pltpu
from jax.sharding import Mesh
from jax.sharding import PartitionSpec as P

B = 256
ORB = 12
ATOMS = 21
PAIRS = 128
MODES = 4
MOMENTA = 32
PLANES = 4
LANES = 8
ROWS = 2 * ORB * ORB
HALVES = (ATOMS + 1) // 2

INTERPRET = False


def split(value):
    high = value.astype(jnp.bfloat16)
    low = (value - high.astype(jnp.float32)).astype(jnp.bfloat16)
    return high, low


def split_complex(real, imag):
    real_high, real_low = split(real)
    imag_high, imag_low = split(imag)
    return real_high, real_low, imag_high, imag_low


def left_factors(parts):
    real_high, real_low, imag_high, imag_low = parts
    plain = [real_high, real_high, real_low]
    turned = [imag_high, imag_high, imag_low]
    minus = [-imag_high, -imag_high, -imag_low]
    return (
        jnp.concatenate(plain + minus, axis=1),
        jnp.concatenate(plain + turned, axis=1),
    )


def dot(left, right):
    return lax.dot_general(
        left, right, (((1,), (0,)), ((), ())), preferred_element_type=jnp.float32
    )


def dot_transposed(left, right):
    return lax.dot_general(
        left, right, (((1,), (1,)), ((), ())), preferred_element_type=jnp.float32
    )


def times(left, right_parts, transposed=False):
    for_real, for_imag = left
    real_high, real_low, imag_high, imag_low = right_parts
    axis = 1 if transposed else 0
    product = dot_transposed if transposed else dot
    real_right = jnp.concatenate(
        [real_high, real_low, real_high, imag_high, imag_low, imag_high], axis=axis
    )
    imag_right = jnp.concatenate(
        [imag_high, imag_low, imag_high, real_high, real_low, real_high], axis=axis
    )
    return product(for_real, real_right), product(for_imag, imag_right)


def add(left, right):
    return left[0] + right[0], left[1] + right[1]


def grid_of(axis, shape=(B, B)):
    return lax.broadcasted_iota(jnp.int32, shape, axis)


def error_and_start(system, bare):
    system_real, system_imag = system
    bare_real, bare_imag = bare
    identity = (grid_of(0) == grid_of(1)).astype(jnp.float32)
    diag_real = jnp.sum(bare_real * identity, axis=0, keepdims=True)
    diag_imag = jnp.sum(bare_imag * identity, axis=0, keepdims=True)
    modulus = diag_real * diag_real + diag_imag * diag_imag
    row_real = diag_real / modulus
    row_imag = -diag_imag / modulus
    column_real = jnp.sum(identity * row_real, axis=1, keepdims=True)
    column_imag = jnp.sum(identity * row_imag, axis=1, keepdims=True)
    error_real = identity - (column_real * system_real - column_imag * system_imag)
    error_imag = -(column_real * system_imag + column_imag * system_real)
    plus_real = identity + error_real
    start = (
        plus_real * row_real - error_imag * row_imag,
        plus_real * row_imag + error_imag * row_real,
    )
    return (error_real, error_imag), start


def inverse_of(system, bare):
    error, start = error_and_start(system, bare)
    error_parts = split_complex(*error)
    squared = times(left_factors(error_parts), error_parts)
    return two_more(squared, start)


def two_more(squared, start):
    squared_parts = split_complex(*squared)
    squared_left = left_factors(squared_parts)
    first = add(start, times(squared_left, split_complex(*start)))
    fourth = times(squared_left, squared_parts)
    fourth_left = left_factors(split_complex(*fourth))
    return add(first, times(fourth_left, split_complex(*first)))


def contact_of(system, coupling):
    error, start = error_and_start(system, system)
    error_parts = split_complex(*error)
    coupling_parts = split_complex(*coupling)
    right = times(left_factors(split_complex(*start)), coupling_parts, transposed=True)
    squared_parts = split_complex(*times(left_factors(error_parts), error_parts))
    fourth = times(left_factors(squared_parts), squared_parts)
    left = add(coupling, times(left_factors(coupling_parts), squared_parts))
    left = add(left, times(left_factors(split_complex(*left)), split_complex(*fourth)))
    return times(left_factors(split_complex(*left)), split_complex(*right))


def first_kernel(
    energy_ref,
    device_hbm,
    lead_hbm,
    coupling_hbm,
    pair_ref,
    system_ref,
    green_ref,
    blocks_ref,
    rows_ref,
    device_ref,
    lead_ref,
    coupling_ref,
    semaphores,
):
    lead_copy = pltpu.make_async_copy(lead_hbm.at[0], lead_ref, semaphores.at[0])
    coupling_copy = pltpu.make_async_copy(coupling_hbm.at[0], coupling_ref, semaphores.at[1])
    device_copy = pltpu.make_async_copy(device_hbm.at[0], device_ref, semaphores.at[2])
    lead_copy.start()
    coupling_copy.start()
    device_copy.start()
    energy = energy_ref[0]
    scaled_identity = jnp.where(grid_of(0) == grid_of(1), energy, 0.0)
    lead_copy.wait()
    coupling_copy.wait()
    lead = (scaled_identity - lead_ref[0], -lead_ref[1])
    contact = contact_of(lead, (coupling_ref[0], coupling_ref[1]))
    device_copy.wait()
    bare = (scaled_identity - device_ref[0], -device_ref[1])
    system = (bare[0] - contact[0], bare[1] - contact[1])
    system_ref[0] = system[0]
    system_ref[1] = system[1]
    green = inverse_of(system, bare)
    green_ref[0] = green[0]
    green_ref[1] = green[1]
    take_blocks(green, pair_ref, rows_ref)
    shards = blocks_ref.shape[0]
    shard_rows = ROWS // shards
    for row in range(ROWS):
        place = (row % shard_rows) * PAIRS
        blocks_ref[row // shard_rows, :, place : place + PAIRS] = rows_ref[row : row + 1, :]


def take_blocks(green, pair_ref, rows_ref):
    real_high, real_low = split(green[0])
    imag_high, imag_low = split(green[1])
    left = jnp.concatenate(
        [
            jnp.concatenate([real_high, real_low], axis=1),
            jnp.concatenate([imag_high, imag_low], axis=1),
        ],
        axis=0,
    )
    row_atom = pair_ref[0:1, :]
    column_atom = pair_ref[1:2, :]
    row_half = row_atom // 2
    row_odd = (row_atom - 2 * row_half) == 1
    row_half = jnp.concatenate([row_half, row_half], axis=1)
    row_odd = jnp.concatenate([row_atom, row_atom], axis=1) - 2 * row_half == 1
    offset = grid_of(0, (B, PAIRS)) - ORB * column_atom
    for first in range(0, ORB, 2):
        pick = jnp.concatenate(
            [(offset == first).astype(jnp.bfloat16), (offset == first + 1).astype(jnp.bfloat16)],
            axis=1,
        )
        columns = dot(left, jnp.concatenate([pick, pick], axis=0))
        for part in range(2):
            found = jnp.zeros((2 * ORB, 2 * PAIRS), jnp.float32)
            for half in range(HALVES):
                begin = part * B + 2 * ORB * half
                if half == HALVES - 1:
                    piece = jnp.concatenate(
                        [columns[begin : begin + 16], jnp.zeros((8, 2 * PAIRS), jnp.float32)], axis=0
                    )
                else:
                    piece = columns[begin : begin + 2 * ORB]
                found = jnp.where(row_half == half, piece, found)
            chosen = jnp.where(row_odd, found[ORB:], found[:ORB])
            for side in range(2):
                row = (part * ORB + first + side) * ORB
                rows_ref[row : row + ORB, :] = chosen[:, side * PAIRS : (side + 1) * PAIRS]


def place_blocks(values, pair_ref):
    row_atom = pair_ref[0:1, :]
    column_atom = pair_ref[1:2, :]
    row_half = row_atom // 2
    row_odd = row_atom - 2 * row_half
    identity = grid_of(0, (PAIRS, PAIRS)) == grid_of(1, (PAIRS, PAIRS))
    column_of = jnp.sum(
        jnp.where(identity, (ORB * column_atom).astype(jnp.float32), 0.0), axis=1, keepdims=True
    ).astype(jnp.int32)
    offset = grid_of(1, (PAIRS, B)) - column_of
    pick = jnp.concatenate(
        [(offset == column).astype(jnp.bfloat16) for column in range(ORB)], axis=0
    )
    results = []
    for part in range(2):
        highs = []
        lows = []
        for column in range(ORB):
            row = (part * ORB + column) * ORB
            block = values[row : row + ORB, :]
            both = jnp.concatenate(
                [jnp.where(row_odd == 0, block, 0.0), jnp.where(row_odd == 1, block, 0.0)], axis=0
            )
            pieces = []
            for half in range(HALVES):
                piece = jnp.where(row_half == half, both, 0.0)
                pieces.append(piece[:16] if half == HALVES - 1 else piece)
            spread = jnp.concatenate(pieces, axis=0)
            high, low = split(spread)
            highs.append(high)
            lows.append(low)
        left = jnp.concatenate(highs + lows, axis=1)
        results.append(dot(left, jnp.concatenate([pick, pick], axis=0)))
    return results


def last_kernel(system_ref, green_ref, blocks_ref, pair_ref, out_ref, rows_ref):
    shard_rows = ROWS // blocks_ref.shape[0]
    for row in range(ROWS):
        place = (row % shard_rows) * PAIRS
        rows_ref[row : row + 1, :] = blocks_ref[row // shard_rows, :, place : place + PAIRS]
    scattering = place_blocks(rows_ref, pair_ref)
    second = (system_ref[0] - scattering[0], system_ref[1] - scattering[1])
    green = (green_ref[0], green_ref[1])
    identity = (grid_of(0) == grid_of(1)).astype(jnp.float32)
    product = times(left_factors(split_complex(*green)), split_complex(*second))
    residual = (identity - product[0], -product[1])
    final = two_more(residual, green)
    out_ref[0, 0, 0] = final[0]
    out_ref[0, 0, 1] = final[1]


def vmem(count):
    return [pl.BlockSpec(memory_space=pltpu.VMEM)] * count


def near_core(array):
    return array if INTERPRET else pltpu.with_memory_space_constraint(array, pltpu.VMEM)


def near_shape(*shape):
    return jax.ShapeDtypeStruct(shape, jnp.float32) if INTERPRET else pltpu.VMEM(shape, jnp.float32)


def first_call(energy, device_hamiltonian, lead_hamiltonian, lead_coupling, pair_atoms, shards):
    shape = near_shape(2, B, B)
    blocks = near_shape(shards, 1, ROWS // shards * PAIRS)
    return pl.pallas_call(
        first_kernel,
        out_shape=(shape, shape, blocks),
        in_specs=[pl.BlockSpec(memory_space=pltpu.SMEM)]
        + [pl.BlockSpec(memory_space=pl.ANY)] * 3
        + vmem(1),
        out_specs=tuple(vmem(3)),
        scratch_shapes=[pltpu.VMEM((ROWS, PAIRS), jnp.float32)]
        + [pltpu.VMEM((2, B, B), jnp.float32)] * 3
        + [pltpu.SemaphoreType.DMA((3,))],
        name="first_round",
        interpret=INTERPRET,
    )(energy, device_hamiltonian, lead_hamiltonian, lead_coupling, pair_atoms)


def last_call(system, green, blocks, pair_atoms):
    return pl.pallas_call(
        last_kernel,
        out_shape=jax.ShapeDtypeStruct((1, 1, 2, B, B), jnp.float32),
        in_specs=vmem(4),
        out_specs=pl.BlockSpec(memory_space=pltpu.VMEM),
        scratch_shapes=[pltpu.VMEM((ROWS, PAIRS), jnp.float32)],
        compiler_params=pltpu.CompilerParams(

        ),
        name="second_round",
        interpret=INTERPRET,
    )(near_core(system), near_core(green), near_core(blocks), pair_atoms)


def exchange(array, axes):
    return lax.all_to_all(array, axes, split_axis=0, concat_axis=0, tiled=True)


def slab_sum_kernel(arrived_ref, out_ref):
    members = arrived_ref.shape[0] // PLANES
    width = arrived_ref.shape[2]
    for plane in range(PLANES):
        total = arrived_ref[plane * members]
        for member in range(1, members):
            total = total + arrived_ref[plane * members + member]
        out_ref[:, plane * width : (plane + 1) * width] = total


def pair_kernel(own_ref, arrived_ref, out_ref):
    out_ref[...] = own_ref[...] + arrived_ref[...]


def copies_kernel(own_ref, arrived_ref, out_ref):
    total = own_ref[...] + arrived_ref[...]
    for copy in range(out_ref.shape[0]):
        out_ref[copy] = total


def convolve_kernel(
    lane_ref, shift_ref, occupation_ref, coupling_ref, arrived_ref, out_ref, rows_ref
):
    lanes = arrived_ref.shape[0]
    planes = PLANES
    stacked = arrived_ref.shape[2] // PAIRS
    rows = stacked // planes
    for lane in range(lanes):
        for row in range(stacked):
            place = lane * stacked + row
            rows_ref[place : place + 1, :] = arrived_ref[lane, :, row * PAIRS : (row + 1) * PAIRS]
    copies = out_ref.shape[0] // planes
    energies = lanes * planes
    source = lax.broadcasted_iota(jnp.int32, (energies, PAIRS), 0)
    weights = []
    for plane in range(planes):
        target = plane * lanes + lane_ref[0]
        total = jnp.zeros((energies, PAIRS), jnp.float32)
        for mode in range(MODES):
            occupied = occupation_ref[mode]
            shift = shift_ref[mode]
            factor = jnp.where(source == target - shift, occupied, 0.0) + jnp.where(
                source == target + shift, occupied + 1.0, 0.0
            )
            total = total + factor * coupling_ref[mode : mode + 1, :]
        weights.append(total / MOMENTA)
    results = [jnp.zeros((rows, PAIRS), jnp.float32) for _ in range(planes)]
    for lane in range(lanes):
        for plane in range(planes):
            begin = lane * stacked + plane * rows
            piece = rows_ref[begin : begin + rows, :]
            energy = plane * lanes + lane
            for target in range(planes):
                results[target] = results[target] + weights[target][energy : energy + 1, :] * piece
    for plane in range(planes):
        for row in range(rows):
            for copy in range(copies):
                out_ref[plane * copies + copy, :, row * PAIRS : (row + 1) * PAIRS] = results[plane][
                    row : row + 1
                ]


def kernel_call(kernel, name, shape, *arguments, scalars=0, scratch=()):
    arguments = arguments[:scalars] + tuple(
        near_core(argument) for argument in arguments[scalars:]
    )
    return pl.pallas_call(
        kernel,
        out_shape=near_shape(*shape),
        in_specs=[pl.BlockSpec(memory_space=pltpu.SMEM)] * scalars
        + vmem(len(arguments) - scalars),
        out_specs=vmem(1)[0],
        scratch_shapes=[pltpu.VMEM(extent, jnp.float32) for extent in scratch],
        name=name,
        interpret=INTERPRET,
    )(*arguments)


def per_device(
    device_hamiltonian,
    lead_hamiltonian,
    lead_coupling,
    pair_atoms,
    phonon_shift,
    occupation,
    phonon_coupling,
):
    slab = PLANES * lax.axis_size("x") * lax.axis_size("core")
    energy_index = lax.axis_index(("y", "z_lo"))
    energy = -1.0 + 2.0 * (energy_index.astype(jnp.float32) + 0.5) / (PLANES * LANES)
    system, green, blocks = first_call(
        energy[None], device_hamiltonian, lead_hamiltonian, lead_coupling, pair_atoms, slab
    )
    arrived = exchange(blocks, ("y", "x", "core"))
    rows = PLANES * ROWS // slab
    summed = kernel_call(slab_sum_kernel, "slab_sum", (1, rows * PAIRS), arrived)
    near = lax.ppermute(summed, "z_hi", [(0, 3), (3, 0), (1, 2), (2, 1)])
    paired = kernel_call(pair_kernel, "pair_sum", (1, rows * PAIRS), summed, near)
    far = lax.ppermute(paired, "z_hi", [(0, 1), (1, 0), (2, 3), (3, 2)])
    copies = kernel_call(copies_kernel, "column_sum", (LANES, 1, rows * PAIRS), paired, far)
    arrived = exchange(copies, "z_lo")
    spread = kernel_call(
        convolve_kernel,
        "phonon_sum",
        blocks.shape,
        lax.axis_index("z_lo")[None],
        phonon_shift,
        occupation,
        phonon_coupling,
        arrived,
        scalars=3,
        scratch=((LANES * rows, PAIRS),),
    )
    arrived = exchange(spread, ("y", "x", "core"))
    return last_call(system, green, arrived, pair_atoms)


def solution(mesh):
    momentum = ("x", "z_hi", "core")
    split_mesh = Mesh(mesh.devices.reshape(PLANES, LANES, 4, 4, 2), ("y", "z_lo") + momentum)
    return jax.shard_map(
        per_device,
        mesh=split_mesh,
        in_specs=(P(momentum),) * 3 + (P(),) * 4,
        out_specs=P(("y", "z_lo"), momentum),
        check_vma=False,
    )
```

```python
import jax
import jax.numpy as jnp
from jax import lax
from jax.experimental import pallas as pl
from jax.experimental.pallas import tpu as pltpu
from jax.sharding import Mesh
from jax.sharding import PartitionSpec as P

B = 256
ORB = 12
ATOMS = 21
PAIRS = 128
MODES = 4
MOMENTA = 32
PLANES = 4
LANES = 8
ROWS = 2 * ORB * ORB
HALVES = (ATOMS + 1) // 2

INTERPRET = False


def split(value):
    high = value.astype(jnp.bfloat16)
    low = (value - high.astype(jnp.float32)).astype(jnp.bfloat16)
    return high, low


def split_complex(real, imag):
    real_high, real_low = split(real)
    imag_high, imag_low = split(imag)
    return real_high, real_low, imag_high, imag_low


def left_factors(parts):
    real_high, real_low, imag_high, imag_low = parts
    plain = [real_high, real_high, real_low]
    turned = [imag_high, imag_high, imag_low]
    minus = [-imag_high, -imag_high, -imag_low]
    return (
        jnp.concatenate(plain + minus, axis=1),
        jnp.concatenate(plain + turned, axis=1),
    )


def dot(left, right):
    return lax.dot_general(
        left, right, (((1,), (0,)), ((), ())), preferred_element_type=jnp.float32
    )


def dot_transposed(left, right):
    return lax.dot_general(
        left, right, (((1,), (1,)), ((), ())), preferred_element_type=jnp.float32
    )


def times(left, right_parts, transposed=False):
    for_real, for_imag = left
    real_high, real_low, imag_high, imag_low = right_parts
    axis = 1 if transposed else 0
    product = dot_transposed if transposed else dot
    real_right = jnp.concatenate(
        [real_high, real_low, real_high, imag_high, imag_low, imag_high], axis=axis
    )
    imag_right = jnp.concatenate(
        [imag_high, imag_low, imag_high, real_high, real_low, real_high], axis=axis
    )
    return product(for_real, real_right), product(for_imag, imag_right)


def add(left, right):
    return left[0] + right[0], left[1] + right[1]


def grid_of(axis, shape=(B, B)):
    return lax.broadcasted_iota(jnp.int32, shape, axis)


def error_and_start(system, bare):
    system_real, system_imag = system
    bare_real, bare_imag = bare
    identity = (grid_of(0) == grid_of(1)).astype(jnp.float32)
    diag_real = jnp.sum(bare_real * identity, axis=0, keepdims=True)
    diag_imag = jnp.sum(bare_imag * identity, axis=0, keepdims=True)
    modulus = diag_real * diag_real + diag_imag * diag_imag
    row_real = diag_real / modulus
    row_imag = -diag_imag / modulus
    column_real = jnp.sum(identity * row_real, axis=1, keepdims=True)
    column_imag = jnp.sum(identity * row_imag, axis=1, keepdims=True)
    error_real = identity - (column_real * system_real - column_imag * system_imag)
    error_imag = -(column_real * system_imag + column_imag * system_real)
    plus_real = identity + error_real
    start = (
        plus_real * row_real - error_imag * row_imag,
        plus_real * row_imag + error_imag * row_real,
    )
    return (error_real, error_imag), start


def inverse_of(system, bare):
    error, start = error_and_start(system, bare)
    error_parts = split_complex(*error)
    squared = times(left_factors(error_parts), error_parts)
    return two_more(squared, start)


def two_more(squared, start):
    squared_parts = split_complex(*squared)
    squared_left = left_factors(squared_parts)
    first = add(start, times(squared_left, split_complex(*start)))
    fourth = times(squared_left, squared_parts)
    fourth_left = left_factors(split_complex(*fourth))
    return add(first, times(fourth_left, split_complex(*first)))


def contact_of(system, coupling):
    error, start = error_and_start(system, system)
    error_parts = split_complex(*error)
    coupling_parts = split_complex(*coupling)
    right = times(left_factors(split_complex(*start)), coupling_parts, transposed=True)
    squared_parts = split_complex(*times(left_factors(error_parts), error_parts))
    fourth = times(left_factors(squared_parts), squared_parts)
    left = add(coupling, times(left_factors(coupling_parts), squared_parts))
    left = add(left, times(left_factors(split_complex(*left)), split_complex(*fourth)))
    return times(left_factors(split_complex(*left)), split_complex(*right))


def first_kernel(
    energy_ref,
    device_hbm,
    lead_hbm,
    coupling_hbm,
    pair_ref,
    system_ref,
    green_ref,
    blocks_ref,
    rows_ref,
    device_ref,
    lead_ref,
    coupling_ref,
    semaphores,
):
    lead_copy = pltpu.make_async_copy(lead_hbm.at[0], lead_ref, semaphores.at[0])
    coupling_copy = pltpu.make_async_copy(coupling_hbm.at[0], coupling_ref, semaphores.at[1])
    device_copy = pltpu.make_async_copy(device_hbm.at[0], device_ref, semaphores.at[2])
    lead_copy.start()
    coupling_copy.start()
    device_copy.start()
    energy = energy_ref[0]
    scaled_identity = jnp.where(grid_of(0) == grid_of(1), energy, 0.0)
    lead_copy.wait()
    coupling_copy.wait()
    lead = (scaled_identity - lead_ref[0], -lead_ref[1])
    contact = contact_of(lead, (coupling_ref[0], coupling_ref[1]))
    device_copy.wait()
    bare = (scaled_identity - device_ref[0], -device_ref[1])
    system = (bare[0] - contact[0], bare[1] - contact[1])
    system_ref[0] = system[0]
    system_ref[1] = system[1]
    green = inverse_of(system, bare)
    green_ref[0] = green[0]
    green_ref[1] = green[1]
    take_blocks(green, pair_ref, rows_ref)
    shards = blocks_ref.shape[0]
    shard_rows = ROWS // shards
    for row in range(ROWS):
        place = (row % shard_rows) * PAIRS
        blocks_ref[row // shard_rows, :, place : place + PAIRS] = rows_ref[row : row + 1, :]


def take_blocks(green, pair_ref, rows_ref):
    real_high, real_low = split(green[0])
    imag_high, imag_low = split(green[1])
    left = jnp.concatenate(
        [
            jnp.concatenate([real_high, real_low], axis=1),
            jnp.concatenate([imag_high, imag_low], axis=1),
        ],
        axis=0,
    )
    row_atom = pair_ref[0:1, :]
    column_atom = pair_ref[1:2, :]
    row_half = row_atom // 2
    row_odd = (row_atom - 2 * row_half) == 1
    row_half = jnp.concatenate([row_half, row_half], axis=1)
    row_odd = jnp.concatenate([row_atom, row_atom], axis=1) - 2 * row_half == 1
    offset = grid_of(0, (B, PAIRS)) - ORB * column_atom
    for first in range(0, ORB, 2):
        pick = jnp.concatenate(
            [(offset == first).astype(jnp.bfloat16), (offset == first + 1).astype(jnp.bfloat16)],
            axis=1,
        )
        columns = dot(left, jnp.concatenate([pick, pick], axis=0))
        for part in range(2):
            found = jnp.zeros((2 * ORB, 2 * PAIRS), jnp.float32)
            for half in range(HALVES):
                begin = part * B + 2 * ORB * half
                if half == HALVES - 1:
                    piece = jnp.concatenate(
                        [columns[begin : begin + 16], jnp.zeros((8, 2 * PAIRS), jnp.float32)], axis=0
                    )
                else:
                    piece = columns[begin : begin + 2 * ORB]
                found = jnp.where(row_half == half, piece, found)
            chosen = jnp.where(row_odd, found[ORB:], found[:ORB])
            for side in range(2):
                row = (part * ORB + first + side) * ORB
                rows_ref[row : row + ORB, :] = chosen[:, side * PAIRS : (side + 1) * PAIRS]


def place_blocks(values, pair_ref):
    row_atom = pair_ref[0:1, :]
    column_atom = pair_ref[1:2, :]
    row_half = row_atom // 2
    row_odd = row_atom - 2 * row_half
    identity = grid_of(0, (PAIRS, PAIRS)) == grid_of(1, (PAIRS, PAIRS))
    column_of = jnp.sum(
        jnp.where(identity, (ORB * column_atom).astype(jnp.float32), 0.0), axis=1, keepdims=True
    ).astype(jnp.int32)
    offset = grid_of(1, (PAIRS, B)) - column_of
    pick = jnp.concatenate(
        [(offset == column).astype(jnp.bfloat16) for column in range(ORB)], axis=0
    )
    results = []
    for part in range(2):
        highs = []
        lows = []
        for column in range(ORB):
            row = (part * ORB + column) * ORB
            block = values[row : row + ORB, :]
            both = jnp.concatenate(
                [jnp.where(row_odd == 0, block, 0.0), jnp.where(row_odd == 1, block, 0.0)], axis=0
            )
            pieces = []
            for half in range(HALVES):
                piece = jnp.where(row_half == half, both, 0.0)
                pieces.append(piece[:16] if half == HALVES - 1 else piece)
            spread = jnp.concatenate(pieces, axis=0)
            high, low = split(spread)
            highs.append(high)
            lows.append(low)
        left = jnp.concatenate(highs + lows, axis=1)
        results.append(dot(left, jnp.concatenate([pick, pick], axis=0)))
    return results


def last_kernel(system_ref, green_ref, blocks_ref, pair_ref, out_ref, rows_ref):
    shard_rows = ROWS // blocks_ref.shape[0]
    for row in range(ROWS):
        place = (row % shard_rows) * PAIRS
        rows_ref[row : row + 1, :] = blocks_ref[row // shard_rows, :, place : place + PAIRS]
    scattering = place_blocks(rows_ref, pair_ref)
    second = (system_ref[0] - scattering[0], system_ref[1] - scattering[1])
    green = (green_ref[0], green_ref[1])
    identity = (grid_of(0) == grid_of(1)).astype(jnp.float32)
    product = times(left_factors(split_complex(*green)), split_complex(*second))
    residual = (identity - product[0], -product[1])
    final = two_more(residual, green)
    out_ref[0, 0, 0] = final[0]
    out_ref[0, 0, 1] = final[1]


def vmem(count):
    return [pl.BlockSpec(memory_space=pltpu.VMEM)] * count


def near_core(array):
    return array if INTERPRET else pltpu.with_memory_space_constraint(array, pltpu.VMEM)


def near_shape(*shape):
    return jax.ShapeDtypeStruct(shape, jnp.float32) if INTERPRET else pltpu.VMEM(shape, jnp.float32)


def first_call(energy, device_hamiltonian, lead_hamiltonian, lead_coupling, pair_atoms, shards):
    shape = near_shape(2, B, B)
    blocks = near_shape(shards, 1, ROWS // shards * PAIRS)
    return pl.pallas_call(
        first_kernel,
        out_shape=(shape, shape, blocks),
        in_specs=[pl.BlockSpec(memory_space=pltpu.SMEM)]
        + [pl.BlockSpec(memory_space=pl.ANY)] * 3
        + vmem(1),
        out_specs=tuple(vmem(3)),
        scratch_shapes=[pltpu.VMEM((ROWS, PAIRS), jnp.float32)]
        + [pltpu.VMEM((2, B, B), jnp.float32)] * 3
        + [pltpu.SemaphoreType.DMA((3,))],
        name="first_round",
        interpret=INTERPRET,
    )(energy, device_hamiltonian, lead_hamiltonian, lead_coupling, pair_atoms)


def last_call(system, green, blocks, pair_atoms):
    return pl.pallas_call(
        last_kernel,
        out_shape=jax.ShapeDtypeStruct((1, 1, 2, B, B), jnp.float32),
        in_specs=vmem(4),
        out_specs=pl.BlockSpec(memory_space=pltpu.VMEM),
        scratch_shapes=[pltpu.VMEM((ROWS, PAIRS), jnp.float32)],
        compiler_params=pltpu.CompilerParams(

        ),
        name="second_round",
        interpret=INTERPRET,
    )(near_core(system), near_core(green), near_core(blocks), pair_atoms)


def exchange(array, axes):
    return lax.all_to_all(array, axes, split_axis=0, concat_axis=0, tiled=True)


def slab_sum_kernel(arrived_ref, out_ref):
    members = arrived_ref.shape[0] // PLANES
    width = arrived_ref.shape[2]
    for plane in range(PLANES):
        total = arrived_ref[plane * members]
        for member in range(1, members):
            total = total + arrived_ref[plane * members + member]
        for copy in range(out_ref.shape[0]):
            out_ref[copy, :, plane * width : (plane + 1) * width] = total


def pair_kernel(own_ref, arrived_ref, out_ref):
    out_ref[...] = own_ref[...] + arrived_ref[...]


def copies_kernel(own_ref, arrived_ref, out_ref):
    total = own_ref[...] + arrived_ref[...]
    width = out_ref.shape[2]
    copies = out_ref.shape[0] // PLANES
    for place in range(out_ref.shape[0]):
        plane = place // copies
        out_ref[place] = total[:, plane * width : (plane + 1) * width]


def convolve_kernel(
    lane_ref, shift_ref, occupation_ref, coupling_ref, arrived_ref, out_ref, rows_ref
):
    lanes = arrived_ref.shape[0]
    planes = PLANES
    stacked = arrived_ref.shape[2] // PAIRS
    rows = stacked // planes
    for lane in range(lanes):
        for row in range(stacked):
            place = lane * stacked + row
            rows_ref[place : place + 1, :] = arrived_ref[lane, :, row * PAIRS : (row + 1) * PAIRS]
    energies = lanes * planes
    source = lax.broadcasted_iota(jnp.int32, (energies, PAIRS), 0)
    weights = []
    for plane in range(planes):
        target = plane * lanes + lane_ref[0]
        total = jnp.zeros((energies, PAIRS), jnp.float32)
        for mode in range(MODES):
            occupied = occupation_ref[mode]
            shift = shift_ref[mode]
            factor = jnp.where(source == target - shift, occupied, 0.0) + jnp.where(
                source == target + shift, occupied + 1.0, 0.0
            )
            total = total + factor * coupling_ref[mode : mode + 1, :]
        weights.append(total / MOMENTA)
    results = [jnp.zeros((rows, PAIRS), jnp.float32) for _ in range(planes)]
    for lane in range(lanes):
        for plane in range(planes):
            begin = lane * stacked + plane * rows
            piece = rows_ref[begin : begin + rows, :]
            energy = plane * lanes + lane
            for target in range(planes):
                results[target] = results[target] + weights[target][energy : energy + 1, :] * piece
    for plane in range(planes):
        for row in range(rows):
            place = (plane * rows + row) * PAIRS
            out_ref[:, place : place + PAIRS] = results[plane][row : row + 1]


def kernel_call(kernel, name, shape, *arguments, scalars=0, scratch=()):
    arguments = arguments[:scalars] + tuple(
        near_core(argument) for argument in arguments[scalars:]
    )
    return pl.pallas_call(
        kernel,
        out_shape=near_shape(*shape),
        in_specs=[pl.BlockSpec(memory_space=pltpu.SMEM)] * scalars
        + vmem(len(arguments) - scalars),
        out_specs=vmem(1)[0],
        scratch_shapes=[pltpu.VMEM(extent, jnp.float32) for extent in scratch],
        name=name,
        interpret=INTERPRET,
    )(*arguments)


def per_device(
    device_hamiltonian,
    lead_hamiltonian,
    lead_coupling,
    pair_atoms,
    phonon_shift,
    occupation,
    phonon_coupling,
):
    slab = PLANES * lax.axis_size("x") * lax.axis_size("core")
    energy_index = lax.axis_index(("y", "z_lo"))
    energy = -1.0 + 2.0 * (energy_index.astype(jnp.float32) + 0.5) / (PLANES * LANES)
    system, green, blocks = first_call(
        energy[None], device_hamiltonian, lead_hamiltonian, lead_coupling, pair_atoms, slab
    )
    arrived = exchange(blocks, ("y", "x", "core"))
    rows = PLANES * ROWS // slab
    copies = kernel_call(slab_sum_kernel, "slab_sum", (LANES, 1, rows * PAIRS), arrived)
    arrived = exchange(copies, "z_lo")
    shifted = kernel_call(
        convolve_kernel,
        "phonon_sum",
        (1, rows * PAIRS),
        lax.axis_index("z_lo")[None],
        phonon_shift,
        occupation,
        phonon_coupling,
        arrived,
        scalars=3,
        scratch=((LANES * rows, PAIRS),),
    )
    near = lax.ppermute(shifted, "z_hi", [(0, 3), (3, 0), (1, 2), (2, 1)])
    paired = kernel_call(pair_kernel, "pair_sum", (1, rows * PAIRS), shifted, near)
    far = lax.ppermute(paired, "z_hi", [(0, 1), (1, 0), (2, 3), (3, 2)])
    spread = kernel_call(copies_kernel, "column_sum", blocks.shape, paired, far)
    arrived = exchange(spread, ("y", "x", "core"))
    return last_call(system, green, arrived, pair_atoms)


def solution(mesh):
    momentum = ("x", "z_hi", "core")
    split_mesh = Mesh(mesh.devices.reshape(PLANES, LANES, 4, 4, 2), ("y", "z_lo") + momentum)
    return jax.shard_map(
        per_device,
        mesh=split_mesh,
        in_specs=(P(momentum),) * 3 + (P(),) * 4,
        out_specs=P(("y", "z_lo"), momentum),
        check_vma=False,
    )
```
